128 devices in a mesh: outer: 2 (over y_hi), inner: 64 (over z, x, y_lo, core).
Axes of the slice: x: 4, y: 4 (y_hi: 2, y_lo: 2; y = y_hi * 2 + y_lo), z: 4, core: 2. Of those that a mesh axis runs over, the one named last changes fastest.
Arguments:
- tile_counts: int32 [128, 4, 1024, 512], P(('outer', 'inner')), may hold values from 0 to 63, as said below
- row_counts: int32 [131072], P(('outer', 'inner')), may hold values from 100 to 19999
- col_counts: int32 [65536], P(('outer', 'inner')), may hold values from 100 to 19999
- row_factors: float32 [131072, 256], P(('outer', 'inner')), may hold values from -1.8 to 1.8
- row_accum: float32 [131072, 256], P(('outer', 'inner')), may hold values from 1 to 10
- col_factors: float32 [65536, 256], P(('outer', 'inner')), may hold values from -1.8 to 1.8
- col_accum: float32 [65536, 256], P(('outer', 'inner')), may hold values from 1 to 10
Outputs:
- rows_final: float32 [131072, 256], P(('outer', 'inner'))
- row_accum_final: float32 [131072, 256], P(('outer', 'inner'))
- cols_final: float32 [65536, 256], P(('outer', 'inner'))
- col_accum_final: float32 [65536, 256], P(('outer', 'inner'))
The draws below stay inside these ranges and needn't reach their ends.
Inputs may be any that keep to these rules, and one draw needn't show every extreme that they name: `tile_counts`: Co-occurrence counts; about half of them are zero.
All inputs are finite; a program needn't handle non-finite values.
Results may differ from the reference program's by a relative error of at most 0.0003.
Values sent between devices are 32-bit elements; how exact they have to be, the bound alone decides.
No kernel may reach another device: no remote copies, remote signals or barrier semaphores. Data moves between devices by JAX's collectives and lax.ppermute only.
A program may use at most 64 MiB of HBM per device.

```python
import math
import jax
import jax.numpy as jnp
from jax import lax

EMBED = 256
TILE_ROWS = 1024
TILE_COLS = 512
STEPS = 4
ROWS = 131072
COLS = 65536
N_OUTER = 2
N_INNER = 64


def draw_tile_counts(key, part):
    shape = (ROWS // TILE_ROWS, STEPS, TILE_ROWS, TILE_COLS)
    key_first, key_second, key_third = jax.random.split(jax.random.fold_in(key, 7), 3)
    present = jax.random.randint(key_first, shape, 0, 2)
    values = jax.random.randint(key_second, shape, 1, 64)
    counts = present * values
    position = jax.random.randint(key_third, (), 0, TILE_COLS)
    counts = counts.at[0, 0, 0, position].set(63)
    return counts.astype(jnp.int32)


def with_ends(array, key, smallest, largest):
    longest = array.shape.index(max(array.shape))
    spots = []
    for shift in (0, 1):
        where = [jax.random.randint(jax.random.fold_in(key, axis), (), 0, length) for axis, length in enumerate(array.shape)]
        where[longest] = (where[longest] + shift) % array.shape[longest]
        spots.append(tuple(where))
    return array.at[spots[0]].set(smallest).at[spots[1]].set(largest)


def shard_levels(stream_key, extent, shards, low, top_value):
    level = 1.0
    for dim, parts in shards:
        heights = jax.random.uniform(jax.random.fold_in(jax.random.fold_in(stream_key, 6), dim), (parts,), jnp.float32, low / len(shards), top_value / len(shards))
        level = level * jnp.repeat(jnp.exp(heights), extent[dim] // parts).reshape((-1,) + (1,) * (len(extent) - 1 - dim))
    return level


def scatter_about(stream_key, shape, scale, limit, pieces=(), kind=jnp.bfloat16):
    result = jax.random.normal(stream_key, shape, jnp.float32) * scale
    if len(pieces) > 0:
        result = shard_levels(stream_key, shape, pieces, -0.22, 0.18) * result
    return jnp.clip(result, min=-limit, max=limit).astype(kind)


def setup_inputs(seed: int = 0) -> dict:
    key_list = jax.random.split(jax.random.key(seed), 8)
    return {
        "tile_counts": draw_tile_counts(jax.random.fold_in(key_list[7], 71), 0),
        "row_counts": with_ends(jax.random.randint(key_list[1], (ROWS,), 100, 20000), jax.random.fold_in(key_list[1], 1), 100, 19999).astype(jnp.int32),
        "col_counts": with_ends(jax.random.randint(key_list[2], (COLS,), 100, 20000), jax.random.fold_in(key_list[2], 1), 100, 19999).astype(jnp.int32),
        "row_factors": scatter_about(key_list[3], (ROWS, EMBED), 0.3, 1.8, ((0, 128),), jnp.float32),
        "row_accum": jnp.clip(jnp.exp(math.log(10.0) - 2.3025851 * jax.random.uniform(key_list[4], (ROWS, EMBED), jnp.float32) ** shard_levels(key_list[4], (ROWS, EMBED), ((0, 128),), -0.2, 0.2)), 1.0, 10.0),
        "col_factors": scatter_about(key_list[5], (COLS, EMBED), 0.3, 1.8, ((0, 128),), jnp.float32),
        "col_accum": jnp.clip(jnp.exp(math.log(10.0) - 2.3025851 * jax.random.uniform(key_list[6], (COLS, EMBED), jnp.float32) ** shard_levels(key_list[6], (COLS, EMBED), ((0, 128),), -0.2, 0.2)), 1.0, 10.0),
    }


LOG_TOTAL = 17.0
LEARNING = 0.05
HIGHEST = lax.Precision.HIGHEST

def local_terms(count_tile, row_logs):
    count_float = count_tile.astype(jnp.float32)
    positive = count_tile > 0
    offset = jnp.log(jnp.maximum(count_float, 1.0)) - row_logs[:, None] + LOG_TOTAL
    confidence = 0.1 + 0.25 * jnp.sqrt(count_float)
    return (offset, confidence, positive)

def error_terms(scores, offset, confidence, positive, col_logs):
    gap = scores - (offset - col_logs[None, :])
    return jnp.where(positive, confidence * gap, jax.nn.sigmoid(gap))

def tile_update(offset, confidence, positive, col_logs, row_vectors, row_sums, col_vectors, col_sums):
    scores = lax.dot_general(row_vectors, col_vectors, (((1,), (1,)), ((), ())), precision=HIGHEST, preferred_element_type=jnp.float32)
    errors = error_terms(scores, offset, confidence, positive, col_logs)
    row_grad = jnp.dot(errors, col_vectors, precision=HIGHEST, preferred_element_type=jnp.float32)
    row_sums = row_sums + row_grad * row_grad
    row_vectors = row_vectors - LEARNING * row_grad / jnp.sqrt(row_sums)
    scores = lax.dot_general(row_vectors, col_vectors, (((1,), (1,)), ((), ())), precision=HIGHEST, preferred_element_type=jnp.float32)
    errors = error_terms(scores, offset, confidence, positive, col_logs)
    col_grad = lax.dot_general(errors, row_vectors, (((0,), (0,)), ((), ())), precision=HIGHEST, preferred_element_type=jnp.float32)
    col_sums = col_sums + col_grad * col_grad
    col_vectors = col_vectors - LEARNING * col_grad / jnp.sqrt(col_sums)
    return (row_vectors, row_sums, col_vectors, col_sums)

def one_place(packed):
    count_tile, row_logs, col_logs, row_vectors, row_sums, col_vectors, col_sums = packed
    offset, confidence, positive = local_terms(count_tile, row_logs)
    return tile_update(offset, confidence, positive, col_logs, row_vectors, row_sums, col_vectors, col_sums)

def move_block(moving, across):
    grid = moving.reshape((N_OUTER, N_INNER) + moving.shape[1:])
    grid = jnp.roll(grid, 1, axis=1)
    grid = jnp.roll(grid, across, axis=0)
    return grid.reshape(moving.shape)

def reference(tile_counts, row_counts, col_counts, row_factors, row_accum, col_factors, col_accum):
    places = N_OUTER * N_INNER
    row_logs = jnp.log(row_counts.astype(jnp.float32)).reshape(places, TILE_ROWS)
    col_logs = jnp.log(col_counts.astype(jnp.float32)).reshape(places, TILE_COLS)
    row_vectors = row_factors.reshape(places, TILE_ROWS, EMBED)
    row_sums = row_accum.reshape(places, TILE_ROWS, EMBED)
    col_vectors = col_factors.reshape(places, TILE_COLS, EMBED)
    col_sums = col_accum.reshape(places, TILE_COLS, EMBED)
    for step_index in range(STEPS):
        results = lax.map(one_place, (tile_counts[:, step_index], row_logs, col_logs, row_vectors, row_sums, col_vectors, col_sums))
        row_vectors, row_sums, col_vectors, col_sums = results
        if step_index + 1 < STEPS:
            across = 1 if step_index + 1 == STEPS // 2 else 0
            col_vectors = move_block(col_vectors, across)
            col_sums = move_block(col_sums, across)
            col_logs = move_block(col_logs, across)
    return (row_vectors.reshape(ROWS, EMBED), row_sums.reshape(ROWS, EMBED), col_vectors.reshape(COLS, EMBED), col_sums.reshape(COLS, EMBED))
```

```python
import jax
import jax.numpy as jnp
from jax import lax
from jax.sharding import PartitionSpec as P

LOG_TOTAL = 17.0
LEARNING = 0.05
HIGH = lax.Precision.HIGH


def local_terms(count_tile, row_logs):
    count_float = count_tile.astype(jnp.float32)
    positive = count_tile > 0
    offset = jnp.log(jnp.maximum(count_float, 1.0)) - row_logs[:, None] + LOG_TOTAL
    confidence = 0.1 + 0.25 * jnp.sqrt(count_float)
    return (offset, confidence, positive)


def error_terms(scores, offset, confidence, positive, col_logs):
    gap = scores - (offset - col_logs[None, :])
    return jnp.where(positive, confidence * gap, jax.nn.sigmoid(gap))


def dot(a, b, ca, cb):
    return lax.dot_general(
        a, b, (((ca,), (cb,)), ((), ())), precision=HIGH, preferred_element_type=jnp.float32
    )


def body(tile_counts, row_counts, col_counts, row_factors, row_accum, col_factors, col_accum):
    total_steps = tile_counts.shape[1]
    halfway = total_steps // 2
    n_outer, n_inner = lax.axis_size("outer"), lax.axis_size("inner")

    def move(block, across):
        route = [
            (o * n_inner + i, (o + across) % n_outer * n_inner + (i + 1) % n_inner)
            for o in range(n_outer)
            for i in range(n_inner)
        ]
        return lax.ppermute(block, ("outer", "inner"), route)

    row_logs = jnp.log(row_counts.astype(jnp.float32))
    col_logs = jnp.log(col_counts.astype(jnp.float32))
    W, A, C, B = row_factors, row_accum, col_factors, col_accum
    for step in range(total_steps):
        offset, confidence, positive = local_terms(tile_counts[0, step], row_logs)
        e = error_terms(dot(W, C, 1, 1), offset, confidence, positive, col_logs)
        g = dot(e, C, 1, 0)
        A = A + g * g
        W = W - LEARNING * g / jnp.sqrt(A)
        e = error_terms(dot(W, C, 1, 1), offset, confidence, positive, col_logs)
        h = dot(e, W, 0, 0)
        B = B + h * h
        C = C - LEARNING * h / jnp.sqrt(B)
        if step + 1 < total_steps:
            across = int(step + 1 == halfway)
            col_logs = move(col_logs, across)
            C = move(C, across)
            C, B = lax.optimization_barrier((C, B))
            B = move(B, across)
    return (W, A, C, B)


def solution(mesh):
    both = ("outer", "inner")
    return jax.shard_map(
        body,
        mesh=mesh,
        in_specs=(P(both, None, None, None), P(both), P(both)) + (P(both, None),) * 4,
        out_specs=(P(both, None),) * 4,
        check_vma=False,
    )
```

```python
import functools

import jax
import jax.numpy as jnp
from jax import lax
from jax.experimental import pallas as pl
from jax.experimental.pallas import tpu as pltpu
from jax.sharding import PartitionSpec as P

LOG_TOTAL = 17.0
LEARNING = 0.05
CHUNK = 512
f32 = jnp.float32
MIB = 28


def dot(a, b, ca, cb):
    return lax.dot_general(
        a, b, (((ca,), (cb,)), ((), ())), precision=lax.Precision.HIGH, preferred_element_type=f32
    )


def adagrad(value, total, grad):
    total = total + grad * grad
    return value - LEARNING * (grad * lax.rsqrt(total)), total


def fetches(pairs, sems):
    copies = [pltpu.make_async_copy(src, dst, sems.at[i]) for i, (src, dst) in enumerate(pairs)]
    for copy in copies:
        copy.start()
    return copies


def chunks(n):
    return [pl.ds(start, CHUNK) for start in range(0, n, CHUNK)]


def tile_pass(before, x_buf, rows_ref, col_logs, C, W_ref, A_ref, Wo_ref, Ao_ref, after):
    row_logs = jnp.log(rows_ref[...].astype(f32)).T - LOG_TOTAL
    per = CHUNK // row_logs.shape[0]
    grad = None
    for i, rows in enumerate(chunks(x_buf.shape[0])):
        before(i)
        x = x_buf[rows, :]
        positive = x > 0
        m = jnp.maximum(x.astype(f32), 1.0)
        logs = [row_logs[:, j : j + 1] for j in range(i * per, (i + 1) * per)]
        target = (jnp.log(m) - jnp.concatenate(logs, axis=0)) - col_logs
        confidence = 0.1 + 0.25 * (m * lax.rsqrt(m))

        def errors(z):
            gap = z - target
            return jnp.where(positive, confidence * gap, 0.5 * jnp.tanh(0.5 * gap) + 0.5)

        W = W_ref[rows, :]
        g = dot(errors(dot(W, C, 1, 1)), C, 1, 0)
        W, A = adagrad(W, A_ref[rows, :], g)
        Ao_ref[rows, :] = A
        Wo_ref[rows, :] = W
        after(i)
        part = dot(W, errors(dot(W, C, 1, 1)), 0, 0)
        grad = part if grad is None else grad + part
    return grad.T


def first_kernel(
    x_hbm, rows_ref, cols_ref, W_hbm, A_hbm, C_hbm, B_hbm,
    Wo_ref, Ao_ref, Co_ref, Bo_ref, x_buf, W_buf, A_buf, C_buf, B_buf, sems,
):
    n, width = C_buf.shape
    parts = chunks(x_buf.shape[0])
    pairs = [(C_hbm, C_buf)]
    for rows in parts:
        pairs.append((W_hbm.at[rows], W_buf.at[rows]))
        pairs.append((x_hbm.at[0, 0, rows], x_buf.at[rows]))
        pairs.append((A_hbm.at[rows], A_buf.at[rows]))
    pairs.append((B_hbm, B_buf))
    copies = fetches(pairs, sems)
    col_logs = jnp.log(cols_ref[...].astype(f32))
    copies[0].wait()
    C = C_buf[...]

    def before(i):
        for copy in copies[1 + 3 * i : 4 + 3 * i]:
            copy.wait()

    h = tile_pass(
        before, x_buf, rows_ref, col_logs, C, W_buf, A_buf, Wo_ref, Ao_ref, lambda i: None
    )
    copies[-1].wait()
    Co_ref[:n, :], Bo_ref[...] = adagrad(C, B_buf[...], h)
    logs = [jnp.broadcast_to(col_logs[:, i : i + width], (8, width)) for i in range(0, n, width)]
    Co_ref[n:, :] = jnp.concatenate(logs, axis=0)


def step_kernel(step, x_hbm, rows_ref, M_ref, W_ref, A_ref, Wo_ref, Ao_ref, h_ref, x_buf, sems):
    n = h_ref.shape[0]
    parts = chunks(x_buf.shape[0])
    copies = fetches([(x_hbm.at[0, step, rows], x_buf.at[rows]) for rows in parts], sems)
    logs = [M_ref[i : i + 1, :] for i in range(n, M_ref.shape[0], 8)]
    col_logs = jnp.concatenate(logs, axis=1)
    h_ref[...] = tile_pass(
        lambda i: copies[i].wait(), x_buf, rows_ref, col_logs, M_ref[:n, :],
        W_ref, A_ref, Wo_ref, Ao_ref, lambda i: None,
    )


def last_kernel(
    step, x_hbm, rows_ref, M_ref, W_ref, A_ref, Wo_hbm, Ao_hbm, h_ref, x_buf, W_buf, A_buf, sems, out_sems
):
    n = h_ref.shape[0]
    parts = chunks(x_buf.shape[0])
    copies = fetches([(x_hbm.at[0, step, rows], x_buf.at[rows]) for rows in parts], sems)
    logs = [M_ref[i : i + 1, :] for i in range(n, M_ref.shape[0], 8)]
    col_logs = jnp.concatenate(logs, axis=1)
    stores = []

    def after(i):
        rows = parts[i]
        pairs = [(W_buf.at[rows], Wo_hbm.at[rows]), (A_buf.at[rows], Ao_hbm.at[rows])]
        stores.extend(fetches(pairs, out_sems.at[i]))

    h_ref[...] = tile_pass(
        lambda i: copies[i].wait(), x_buf, rows_ref, col_logs, M_ref[:n, :],
        W_ref, A_ref, W_buf, A_buf, after,
    )
    for copy in stores:
        copy.wait()


def update_kernel(h_ref, M_ref, B_ref, Mo_ref, Bo_ref):
    n = h_ref.shape[0]
    C, Bo_ref[...] = adagrad(M_ref[:n, :], B_ref[...], h_ref[...])
    Mo_ref[:n, :] = C
    if Mo_ref.shape[0] > n:
        Mo_ref[n:, :] = M_ref[n:, :]


def call(kernel, operands, spaces, outs, out_spaces, scratch, mib, name):
    return pl.pallas_call(
        kernel,
        in_specs=[pl.BlockSpec(memory_space=s) for s in spaces],
        out_specs=[pl.BlockSpec(memory_space=s) for s in out_spaces],
        out_shape=[jax.ShapeDtypeStruct(s, f32) for s in outs],
        scratch_shapes=scratch,
        compiler_params=pltpu.CompilerParams(vmem_limit_bytes=mib << 20),
        name=name,
    )(*operands)


def body(tile_counts, row_counts, col_counts, row_factors, row_accum, col_factors, col_accum):
    steps = tile_counts.shape[1]
    n_outer, n_inner = lax.axis_size("outer"), lax.axis_size("inner")

    def move(block, across):
        route = [
            (o * n_inner + i, (o + across) % n_outer * n_inner + (i + 1) % n_inner)
            for o in range(n_outer)
            for i in range(n_inner)
        ]
        return lax.ppermute(block, ("outer", "inner"), route)

    rows = row_counts.reshape(-1, 128)
    cols = col_counts.reshape(1, -1)
    wide, tall = row_factors.shape, col_factors.shape
    message = (tall[0] + 8 * (tall[0] // tall[1]), tall[1])
    hbm = [tile_counts, row_factors, row_accum, col_factors, col_accum]
    hbm = [pltpu.with_memory_space_constraint(a, pltpu.HBM) for a in hbm]
    tile_counts, row_factors, row_accum, col_factors, col_accum = hbm
    V, H, DMA = pltpu.VMEM, pltpu.HBM, pltpu.SemaphoreType.DMA
    tile = V(tile_counts.shape[2:], jnp.int32)
    n = wide[0] // CHUNK
    W, A, M, B = call(
        first_kernel,
        (tile_counts, rows, cols, row_factors, row_accum, col_factors, col_accum),
        [H, V, V, H, H, H, H], [wide, wide, message, tall], [V] * 4,
        [tile, V(wide, f32), V(wide, f32), V(tall, f32), V(tall, f32), DMA((3 * n + 2,))],
        MIB, "first",
    )
    for step in range(1, steps):
        across = int(step == steps // 2)
        M = move(M, across)
        B = move(B, across)
        last = step + 1 == steps
        if last:
            kernel, out_space = last_kernel, H
            scratch = [V(wide, f32), V(wide, f32), DMA((n,)), DMA((n, 2))]
        else:
            kernel, out_space, scratch = step_kernel, V, [DMA((n,))]
        W, A, h = call(
            functools.partial(kernel, step), (tile_counts, rows, M, W, A), [H, V, V, V, V],
            [wide, wide, tall], [out_space, out_space, V], [tile] + scratch, MIB, "tile",
        )
        M, B = call(
            update_kernel, (h, M, B), [V] * 3, [tall if last else message, tall], [V] * 2, [], 8, "update"
        )
    return W, A, M, B


def solution(mesh):
    both = ("outer", "inner")
    return jax.shard_map(
        body,
        mesh=mesh,
        in_specs=(P(both, None, None, None), P(both), P(both)) + (P(both, None),) * 4,
        out_specs=(P(both, None),) * 4,
        check_vma=False,
    )
```

```python
import functools

import jax
import jax.numpy as jnp
from jax import lax
from jax.experimental import pallas as pl
from jax.experimental.pallas import tpu as pltpu
from jax.sharding import PartitionSpec as P

LOG_TOTAL = 17.0
LEARNING = 0.05
HALVES = 2
f32 = jnp.float32
V, H, DMA = pltpu.VMEM, pltpu.HBM, pltpu.SemaphoreType.DMA


def dot(a, b, ca, cb):
    return lax.dot_general(
        a, b, (((ca,), (cb,)), ((), ())), precision=lax.Precision.HIGH, preferred_element_type=f32
    )


def adagrad(value, total, grad):
    total = total + grad * grad
    return value - LEARNING * (grad * lax.rsqrt(total)), total


def fetches(pairs, sems):
    copies = [pltpu.make_async_copy(src, dst, sems.at[i]) for i, (src, dst) in enumerate(pairs)]
    for copy in copies:
        copy.start()
    return copies


def row_spans(n, size):
    return [pl.ds(start, size) for start in range(0, n, size)]


def put_terms(x, row_logs, first, t_ref, c_ref, rows):
    m = jnp.maximum(x.astype(f32), 1.0)
    lanes = row_logs.shape[0]
    logs = [row_logs[:, j : j + 1] for j in range(first, first + x.shape[0] // lanes)]
    t_ref[rows, :] = jnp.log(m) - jnp.concatenate(logs, axis=0)
    c_ref[rows, :] = jnp.where(x > 0, 0.1 + 0.25 * (m * lax.rsqrt(m)), 0.0)


def errors(z, target, confidence, col_logs):
    gap = (z - target) + col_logs
    return jnp.where(confidence > 0.0, confidence * gap, 0.5 * jnp.tanh(0.5 * gap) + 0.5)


def shifted_row_logs(rows_ref):
    return jnp.log(rows_ref[...].astype(f32)).T - LOG_TOTAL


def terms_kernel(step, x_hbm, rows_ref, t_ref, c_ref, x_buf, sems):
    spans = row_spans(x_buf.shape[0], 256)
    copies = fetches([(x_hbm.at[0, step, rows], x_buf.at[rows]) for rows in spans], sems)
    row_logs = shifted_row_logs(rows_ref)
    for i, rows in enumerate(spans):
        copies[i].wait()
        put_terms(x_buf[rows, :], row_logs, 2 * i, t_ref, c_ref, rows)


def first_kernel(
    x_hbm, rows_hbm, cols_hbm, W_hbm, A_hbm, C_hbm, B_hbm,
    Wo_ref, Ao_ref, t_ref, c_ref, *rest,
):
    M_refs, B_refs = rest[:HALVES], rest[HALVES : 2 * HALVES]
    x_buf, W_buf, A_buf, rows_buf, cols_buf, sems, out_sems = rest[2 * HALVES :]
    n, width = B_refs[0].shape
    spans = row_spans(x_buf.shape[0], 512)
    pairs = [(cols_hbm, cols_buf), (rows_hbm, rows_buf)]
    pairs += [(C_hbm.at[pl.ds(j * n, n)], M_refs[j].at[pl.ds(0, n)]) for j in range(HALVES)]
    head = len(pairs)
    for rows in spans:
        pairs.append((W_hbm.at[rows], W_buf.at[rows]))
        pairs.append((x_hbm.at[0, 0, rows], x_buf.at[rows]))
        pairs.append((A_hbm.at[rows], A_buf.at[rows]))
    copies = fetches(pairs, sems)
    late = fetches([(B_hbm.at[pl.ds(j * n, n)], B_refs[j]) for j in range(HALVES)], out_sems)
    for copy in copies[:head]:
        copy.wait()
    col_logs = jnp.log(cols_buf[...].astype(f32))
    row_logs = shifted_row_logs(rows_buf)
    for j in range(HALVES):
        M_refs[j][n:, :] = jnp.broadcast_to(col_logs[:, j * n : (j + 1) * n], (8, width))
    C = jnp.concatenate([ref[:n, :] for ref in M_refs], axis=0)
    for i, rows in enumerate(spans):
        for copy in copies[head + 3 * i : head + 3 * i + 3]:
            copy.wait()
        put_terms(x_buf[rows, :], row_logs, 4 * i, t_ref, c_ref, rows)
        W = W_buf[rows, :]
        e = errors(dot(W, C, 1, 1), t_ref[rows, :], c_ref[rows, :], col_logs)
        Wo_ref[rows, :], Ao_ref[rows, :] = adagrad(W, A_buf[rows, :], dot(e, C, 1, 0))
    for copy in late:
        copy.wait()


def half_errors(j, W, t_ref, c_ref, M_ref, rows):
    n = M_ref.shape[1]
    cols = pl.ds(j * n, n)
    C = M_ref[:n, :]
    e = errors(dot(W, C, 1, 1), t_ref[rows, cols], c_ref[rows, cols], M_ref[n : n + 1, :])
    return e, C


def row_part_kernel(j, t_ref, c_ref, M_ref, W_ref, g_ref):
    for rows in row_spans(W_ref.shape[0], 512):
        e, C = half_errors(j, W_ref[rows, :], t_ref, c_ref, M_ref, rows)
        g_ref[rows, :] = dot(e, C, 1, 0)


def row_last_kernel(j, t_ref, c_ref, M_ref, W_ref, A_ref, g_ref, Wo_ref, Ao_ref):
    for rows in row_spans(W_ref.shape[0], 512):
        W = W_ref[rows, :]
        e, C = half_errors(j, W, t_ref, c_ref, M_ref, rows)
        g = g_ref[rows, :] + dot(e, C, 1, 0)
        Wo_ref[rows, :], Ao_ref[rows, :] = adagrad(W, A_ref[rows, :], g)


def col_kernel(j, t_ref, c_ref, M_ref, W_ref, h_ref):
    grad = None
    for rows in row_spans(W_ref.shape[0], 512):
        W = W_ref[rows, :]
        e, _ = half_errors(j, W, t_ref, c_ref, M_ref, rows)
        part = dot(W, e, 0, 0)
        grad = part if grad is None else grad + part
    h_ref[...] = grad.T


def col_store_kernel(j, t_ref, c_ref, M_ref, W_ref, A_ref, h_ref, Wo_hbm, Ao_hbm, sems):
    copies = fetches([(W_ref, Wo_hbm), (A_ref, Ao_hbm)], sems)
    col_kernel(j, t_ref, c_ref, M_ref, W_ref, h_ref)
    for copy in copies:
        copy.wait()


def update_kernel(h_ref, M_ref, B_ref, Mo_ref, Bo_ref):
    n = h_ref.shape[0]
    Mo_ref[:n, :], Bo_ref[...] = adagrad(M_ref[:n, :], B_ref[...], h_ref[...])
    Mo_ref[n:, :] = M_ref[n:, :]


def final_kernel(*refs):
    ins, (Co_ref, Bo_ref) = refs[:-2], refs[-2:]
    n = ins[0].shape[0]
    for j in range(HALVES):
        h_ref, M_ref, B_ref = ins[3 * j : 3 * j + 3]
        rows = pl.ds(j * n, n)
        Co_ref[rows, :], Bo_ref[rows, :] = adagrad(M_ref[:n, :], B_ref[...], h_ref[...])


def call(kernel, operands, spaces, outs, out_spaces, scratch, mib, name):
    return pl.pallas_call(
        kernel,
        in_specs=[pl.BlockSpec(memory_space=s) for s in spaces],
        out_specs=[pl.BlockSpec(memory_space=s) for s in out_spaces],
        out_shape=[jax.ShapeDtypeStruct(s, f32) for s in outs],
        scratch_shapes=scratch,
        compiler_params=pltpu.CompilerParams(vmem_limit_bytes=mib << 20),
        name=name,
    )(*operands)


def body(tile_counts, row_counts, col_counts, row_factors, row_accum, col_factors, col_accum):
    steps = tile_counts.shape[1]
    n_outer, n_inner = lax.axis_size("outer"), lax.axis_size("inner")

    def move(block, across):
        route = [
            (o * n_inner + i, (o + across) % n_outer * n_inner + (i + 1) % n_inner)
            for o in range(n_outer)
            for i in range(n_inner)
        ]
        return lax.ppermute(block, ("outer", "inner"), route)

    rows = row_counts.reshape(-1, 128)
    cols = col_counts.reshape(1, -1)
    hbm = [tile_counts, rows, cols, row_factors, row_accum, col_factors, col_accum]
    hbm = [pltpu.with_memory_space_constraint(a, H) for a in hbm]
    wide, tall = row_factors.shape, col_factors.shape
    tile = tile_counts.shape[2:]
    half = (tall[0] // HALVES, tall[1])
    message = (half[0] + 8, half[1])
    W, A, t, c, *blocks = call(
        first_kernel, hbm, [H] * 7,
        [wide, wide, tile, tile] + [message] * HALVES + [half] * HALVES, [V] * (4 + 2 * HALVES),
        [V(tile, jnp.int32), V(wide, f32), V(wide, f32), V(rows.shape, jnp.int32),
         V(cols.shape, jnp.int32), DMA((4 + 3 * 2,)), DMA((HALVES,))],
        24, "first",
    )
    M, B = blocks[:HALVES], blocks[HALVES:]
    for step in range(steps):
        if step > 0:
            part = call(
                functools.partial(row_part_kernel, 0), (t, c, M[0], W), [V] * 4, [wide], [V], [], 12, "row0"
            )[0]
            W, A = call(
                functools.partial(row_last_kernel, 1), (t, c, M[1], W, A, part), [V] * 6,
                [wide, wide], [V] * 2, [], 12, "row1",
            )
        if step + 1 == steps:
            break
        across = int(step + 1 == steps // 2)
        sent, sums = [], []
        for j in range(HALVES):
            h = call(functools.partial(col_kernel, j), (t, c, M[j], W), [V] * 4, [half], [V], [], 12, "col%d" % j)[0]
            value, total = call(
                update_kernel, (h, M[j], B[j]), [V] * 3, [message, half], [V] * 2, [], 4, "update%d" % j
            )
            sent.append(move(value, across))
            sums.append(total)
        row_tie = lax.optimization_barrier((rows, *sums))[0]
        t, c = call(
            functools.partial(terms_kernel, step + 1), (hbm[0], row_tie), [H, V], [tile, tile], [V] * 2,
            [V(tile, jnp.int32), DMA((4,))], 12, "terms",
        )
        M, B = sent, [move(total, across) for total in sums]
    h0, W_out, A_out = call(
        functools.partial(col_store_kernel, 0), (t, c, M[0], W, A), [V] * 5, [half, wide, wide], [V, H, H],
        [DMA((2,))], 12, "col0",
    )
    h1 = call(functools.partial(col_kernel, 1), (t, c, M[1], W), [V] * 4, [half], [V], [], 12, "col1")[0]
    C, B = call(final_kernel, (h0, M[0], B[0], h1, M[1], B[1]), [V] * 6, [tall, tall], [V] * 2, [], 6, "final")
    return W_out, A_out, C, B


def solution(mesh):
    both = ("outer", "inner")
    return jax.shard_map(
        body,
        mesh=mesh,
        in_specs=(P(both, None, None, None), P(both), P(both)) + (P(both, None),) * 4,
        out_specs=(P(both, None),) * 4,
        check_vma=False,
    )
```

```python
import functools

import jax
import jax.numpy as jnp
from jax import lax
from jax.experimental import pallas as pl
from jax.experimental.pallas import tpu as pltpu
from jax.sharding import PartitionSpec as P

LOG_TOTAL = 17.0
LEARNING = 0.05
HALVES = 2
f32 = jnp.float32
V, H, DMA = pltpu.VMEM, pltpu.HBM, pltpu.SemaphoreType.DMA


def dot(a, b, ca, cb):
    return lax.dot_general(
        a, b, (((ca,), (cb,)), ((), ())), precision=lax.Precision.HIGH, preferred_element_type=f32
    )


def adagrad(value, total, grad):
    total = total + grad * grad
    return value - LEARNING * (grad * lax.rsqrt(total)), total


def fetches(pairs, sems):
    copies = [pltpu.make_async_copy(src, dst, sems.at[i]) for i, (src, dst) in enumerate(pairs)]
    for copy in copies:
        copy.start()
    return copies


def row_spans(n, size):
    return [pl.ds(start, size) for start in range(0, n, size)]


def put_terms(x, row_logs, first, t_ref, c_ref, rows):
    m = jnp.maximum(x.astype(f32), 1.0)
    lanes = row_logs.shape[0]
    logs = [row_logs[:, j : j + 1] for j in range(first, first + x.shape[0] // lanes)]
    t_ref[rows, :] = jnp.log(m) - jnp.concatenate(logs, axis=0)
    c_ref[rows, :] = jnp.where(x > 0, 0.1 + 0.25 * (m * lax.rsqrt(m)), 0.0)


def errors(z, target, confidence, col_logs):
    gap = (z - target) + col_logs
    return jnp.where(confidence > 0.0, confidence * gap, 0.5 * jnp.tanh(0.5 * gap) + 0.5)


def shifted_row_logs(rows_ref):
    return jnp.log(rows_ref[...].astype(f32)).T - LOG_TOTAL


def terms_kernel(step, x_hbm, rows_ref, t_ref, c_ref, x_buf, sems):
    spans = row_spans(x_buf.shape[0], 256)
    copies = fetches([(x_hbm.at[0, step, rows], x_buf.at[rows]) for rows in spans], sems)
    row_logs = shifted_row_logs(rows_ref)
    for i, rows in enumerate(spans):
        copies[i].wait()
        put_terms(x_buf[rows, :], row_logs, 2 * i, t_ref, c_ref, rows)


def first_kernel(
    x_hbm, rows_hbm, cols_hbm, W_hbm, A_hbm, C_hbm, B_hbm,
    Wo_ref, Ao_ref, t_ref, c_ref, *rest,
):
    M_refs, B_refs = rest[:HALVES], rest[HALVES : 2 * HALVES]
    x_buf, W_buf, A_buf, rows_buf, cols_buf, sems, out_sems = rest[2 * HALVES :]
    n, width = B_refs[0].shape
    spans = row_spans(x_buf.shape[0], 512)
    pairs = [(cols_hbm, cols_buf), (rows_hbm, rows_buf)]
    pairs += [(C_hbm.at[pl.ds(j * n, n)], M_refs[j].at[pl.ds(0, n)]) for j in range(HALVES)]
    head = len(pairs)
    for rows in spans:
        pairs.append((W_hbm.at[rows], W_buf.at[rows]))
        pairs.append((x_hbm.at[0, 0, rows], x_buf.at[rows]))
        pairs.append((A_hbm.at[rows], A_buf.at[rows]))
    copies = fetches(pairs, sems)
    late = fetches([(B_hbm.at[pl.ds(j * n, n)], B_refs[j]) for j in range(HALVES)], out_sems)
    for copy in copies[:head]:
        copy.wait()
    col_logs = jnp.log(cols_buf[...].astype(f32))
    row_logs = shifted_row_logs(rows_buf)
    for j in range(HALVES):
        M_refs[j][n:, :] = jnp.broadcast_to(col_logs[:, j * n : (j + 1) * n], (8, width))
    C = jnp.concatenate([ref[:n, :] for ref in M_refs], axis=0)
    for i, rows in enumerate(spans):
        for copy in copies[head + 3 * i : head + 3 * i + 3]:
            copy.wait()
        put_terms(x_buf[rows, :], row_logs, 4 * i, t_ref, c_ref, rows)
        W = W_buf[rows, :]
        e = errors(dot(W, C, 1, 1), t_ref[rows, :], c_ref[rows, :], col_logs)
        Wo_ref[rows, :], Ao_ref[rows, :] = adagrad(W, A_buf[rows, :], dot(e, C, 1, 0))
    for copy in late:
        copy.wait()


def half_errors(j, W, t_ref, c_ref, M_ref, rows):
    n = M_ref.shape[1]
    cols = pl.ds(j * n, n)
    C = M_ref[:n, :]
    e = errors(dot(W, C, 1, 1), t_ref[rows, cols], c_ref[rows, cols], M_ref[n : n + 1, :])
    return e, C


def row_part_kernel(t_ref, c_ref, M_ref, W_ref, g_ref):
    for rows in row_spans(W_ref.shape[0], 256):
        e, C = half_errors(0, W_ref[rows, :], t_ref, c_ref, M_ref, rows)
        g_ref[rows, :] = dot(e, C, 1, 0)


def row_col_kernel(
    size, halves, after, t_ref, c_ref, M0_ref, M1_ref, W_ref, A_ref, g_ref, Wo_ref, Ao_ref, *h_refs
):
    M_refs = (M0_ref, M1_ref)
    grads = [None] * len(halves)
    for rows in row_spans(W_ref.shape[0], size):
        W = W_ref[rows, :]
        e, C = half_errors(1, W, t_ref, c_ref, M1_ref, rows)
        W, A = adagrad(W, A_ref[rows, :], g_ref[rows, :] + dot(e, C, 1, 0))
        Wo_ref[rows, :] = W
        Ao_ref[rows, :] = A
        after(rows)
        for k, j in enumerate(halves):
            part = dot(W, half_errors(j, W, t_ref, c_ref, M_refs[j], rows)[0], 0, 0)
            grads[k] = part if grads[k] is None else grads[k] + part
    for grad, h_ref in zip(grads, h_refs):
        h_ref[...] = grad.T


def last_kernel(*refs):
    ins, (Wo_hbm, Ao_hbm, h0_ref, h1_ref, W_buf, A_buf, sems) = refs[:7], refs[7:]
    stores = []

    def after(rows):
        pairs = [(W_buf.at[rows], Wo_hbm.at[rows]), (A_buf.at[rows], Ao_hbm.at[rows])]
        stores.extend(fetches(pairs, sems.at[len(stores) // 2]))

    row_col_kernel(512, (0, 1), after, *ins, W_buf, A_buf, h0_ref, h1_ref)
    for copy in stores:
        copy.wait()


def col_kernel(j, t_ref, c_ref, M_ref, W_ref, h_ref):
    grad = None
    for rows in row_spans(W_ref.shape[0], 256):
        W = W_ref[rows, :]
        e, _ = half_errors(j, W, t_ref, c_ref, M_ref, rows)
        part = dot(W, e, 0, 0)
        grad = part if grad is None else grad + part
    h_ref[...] = grad.T


def update_kernel(h_ref, M_ref, B_ref, Mo_ref, Bo_ref):
    n = h_ref.shape[0]
    Mo_ref[:n, :], Bo_ref[...] = adagrad(M_ref[:n, :], B_ref[...], h_ref[...])
    Mo_ref[n:, :] = M_ref[n:, :]


def final_kernel(*refs):
    ins, (Co_ref, Bo_ref) = refs[:-2], refs[-2:]
    n = ins[0].shape[0]
    for j in range(HALVES):
        h_ref, M_ref, B_ref = ins[3 * j : 3 * j + 3]
        rows = pl.ds(j * n, n)
        Co_ref[rows, :], Bo_ref[rows, :] = adagrad(M_ref[:n, :], B_ref[...], h_ref[...])


def call(kernel, operands, spaces, outs, out_spaces, scratch, mib, name):
    return pl.pallas_call(
        kernel,
        in_specs=[pl.BlockSpec(memory_space=s) for s in spaces],
        out_specs=[pl.BlockSpec(memory_space=s) for s in out_spaces],
        out_shape=[jax.ShapeDtypeStruct(s, f32) for s in outs],
        scratch_shapes=scratch,
        compiler_params=pltpu.CompilerParams(vmem_limit_bytes=mib << 20),
        name=name,
    )(*operands)


def body(tile_counts, row_counts, col_counts, row_factors, row_accum, col_factors, col_accum):
    steps = tile_counts.shape[1]
    n_outer, n_inner = lax.axis_size("outer"), lax.axis_size("inner")

    def move(block, across):
        route = [
            (o * n_inner + i, (o + across) % n_outer * n_inner + (i + 1) % n_inner)
            for o in range(n_outer)
            for i in range(n_inner)
        ]
        return lax.ppermute(block, ("outer", "inner"), route)

    rows = row_counts.reshape(-1, 128)
    cols = col_counts.reshape(1, -1)
    hbm = [tile_counts, rows, cols, row_factors, row_accum, col_factors, col_accum]
    hbm = [pltpu.with_memory_space_constraint(a, H) for a in hbm]
    wide, tall = row_factors.shape, col_factors.shape
    tile = tile_counts.shape[2:]
    half = (tall[0] // HALVES, tall[1])
    message = (half[0] + 8, half[1])
    W, A, t, c, *blocks = call(
        first_kernel, hbm, [H] * 7,
        [wide, wide, tile, tile] + [message] * HALVES + [half] * HALVES, [V] * (4 + 2 * HALVES),
        [V(tile, jnp.int32), V(wide, f32), V(wide, f32), V(rows.shape, jnp.int32),
         V(cols.shape, jnp.int32), DMA((4 + 3 * 2,)), DMA((HALVES,))],
        24, "first",
    )
    M, B = blocks[:HALVES], blocks[HALVES:]
    for step in range(steps):
        h = None
        if step > 0:
            part = call(row_part_kernel, (t, c, M[0], W), [V] * 4, [wide], [V], [], 12, "row")[0]
            operands = (t, c, M[0], M[1], W, A, part)
            if step + 1 == steps:
                W, A, *grads = call(
                    last_kernel, operands, [V] * 7, [wide, wide, half, half], [H, H, V, V],
                    [V(wide, f32), V(wide, f32), DMA((2, 2))], 20, "last",
                )
                break
            W, A, h = call(
                functools.partial(row_col_kernel, 256, (0,), lambda rows: None), operands, [V] * 7,
                [wide, wide, half], [V] * 3, [], 16, "row_col",
            )
        across = int(step + 1 == steps // 2)
        sent, sums = [], []
        for j in range(HALVES):
            if h is None or j > 0:
                operands = (t, c, M[j], W)
                h = call(functools.partial(col_kernel, j), operands, [V] * 4, [half], [V], [], 12, "col")[0]
            value, total = call(
                update_kernel, (h, M[j], B[j]), [V] * 3, [message, half], [V] * 2, [], 4, "update"
            )
            sent.append(move(value, across))
            sums.append(total)
        row_tie = lax.optimization_barrier((rows, *sums))[0]
        t, c = call(
            functools.partial(terms_kernel, step + 1), (hbm[0], row_tie), [H, V], [tile, tile], [V] * 2,
            [V(tile, jnp.int32), DMA((4,))], 12, "terms",
        )
        M, B = sent, [move(total, across) for total in sums]
    operands = (grads[0], M[0], B[0], grads[1], M[1], B[1])
    C, B = call(final_kernel, operands, [V] * 6, [tall, tall], [V] * 2, [], 6, "final")
    return W, A, C, B


def solution(mesh):
    both = ("outer", "inner")
    return jax.shard_map(
        body,
        mesh=mesh,
        in_specs=(P(both, None, None, None), P(both), P(both)) + (P(both, None),) * 4,
        out_specs=(P(both, None),) * 4,
        check_vma=False,
    )
```

```python
import functools

import jax
import jax.numpy as jnp
from jax import lax
from jax.experimental import pallas as pl
from jax.experimental.pallas import tpu as pltpu
from jax.sharding import PartitionSpec as P


LOG_TOTAL = 17.0
LEARNING = 0.05
HALVES = 2
f32 = jnp.float32
V, H, DMA = pltpu.VMEM, pltpu.HBM, pltpu.SemaphoreType.DMA


def dot(a, b, ca, cb):
    return lax.dot_general(
        a, b, (((ca,), (cb,)), ((), ())), precision=lax.Precision.HIGH, preferred_element_type=f32
    )


def adagrad(value, total, grad):
    total = total + grad * grad
    return value - LEARNING * (grad * lax.rsqrt(total)), total


def fetches(pairs, sems):
    copies = [pltpu.make_async_copy(src, dst, sems.at[i]) for i, (src, dst) in enumerate(pairs)]
    for copy in copies:
        copy.start()
    return copies


def row_spans(n, size):
    return [pl.ds(start, size) for start in range(0, n, size)]


def put_terms(x, row_logs, first, t_ref, c_ref, rows):
    m = jnp.maximum(x.astype(f32), 1.0)
    lanes = row_logs.shape[0]
    logs = [row_logs[:, j : j + 1] for j in range(first, first + x.shape[0] // lanes)]
    t_ref[rows, :] = jnp.log(m) - jnp.concatenate(logs, axis=0)
    c_ref[rows, :] = jnp.where(x > 0, 0.1 + 0.25 * (m * lax.rsqrt(m)), 0.0)


def errors(z, target, confidence, col_logs):
    gap = (z - target) + col_logs
    return jnp.where(confidence > 0.0, confidence * gap, 0.5 * jnp.tanh(0.5 * gap) + 0.5)


def shifted_row_logs(rows_ref):
    return jnp.log(rows_ref[...].astype(f32)).T - LOG_TOTAL


def terms_kernel(step, x_hbm, rows_ref, t_ref, c_ref, x_buf, sems):
    spans = row_spans(x_buf.shape[0], 256)
    copies = fetches([(x_hbm.at[0, step, rows], x_buf.at[rows]) for rows in spans], sems)
    row_logs = shifted_row_logs(rows_ref)
    for i, rows in enumerate(spans):
        copies[i].wait()
        put_terms(x_buf[rows, :], row_logs, 2 * i, t_ref, c_ref, rows)


def first_kernel(
    x_hbm, rows_hbm, cols_hbm, W_hbm, A_hbm, C_hbm, B_hbm,
    Wo_ref, Ao_ref, t_ref, c_ref, *rest,
):
    M_refs, B_refs = rest[:HALVES], rest[HALVES : 2 * HALVES]
    x_buf, W_buf, A_buf, rows_buf, cols_buf, sems, out_sems = rest[2 * HALVES :]
    n, width = B_refs[0].shape
    spans = row_spans(x_buf.shape[0], 512)
    pairs = [(cols_hbm, cols_buf), (rows_hbm, rows_buf)]
    pairs += [(C_hbm.at[pl.ds(j * n, n)], M_refs[j].at[pl.ds(0, n)]) for j in range(HALVES)]
    head = len(pairs)
    for rows in spans:
        pairs.append((W_hbm.at[rows], W_buf.at[rows]))
        pairs.append((x_hbm.at[0, 0, rows], x_buf.at[rows]))
        pairs.append((A_hbm.at[rows], A_buf.at[rows]))
    copies = fetches(pairs, sems)
    late = fetches([(B_hbm.at[pl.ds(j * n, n)], B_refs[j]) for j in range(HALVES)], out_sems)
    for copy in copies[:head]:
        copy.wait()
    col_logs = jnp.log(cols_buf[...].astype(f32))
    row_logs = shifted_row_logs(rows_buf)
    for j in range(HALVES):
        M_refs[j][n:, :] = jnp.broadcast_to(col_logs[:, j * n : (j + 1) * n], (8, width))
    C = jnp.concatenate([ref[:n, :] for ref in M_refs], axis=0)
    for i, rows in enumerate(spans):
        for copy in copies[head + 3 * i : head + 3 * i + 3]:
            copy.wait()
        put_terms(x_buf[rows, :], row_logs, 4 * i, t_ref, c_ref, rows)
        W = W_buf[rows, :]
        e = errors(dot(W, C, 1, 1), t_ref[rows, :], c_ref[rows, :], col_logs)
        Wo_ref[rows, :], Ao_ref[rows, :] = adagrad(W, A_buf[rows, :], dot(e, C, 1, 0))
    for copy in late:
        copy.wait()


def half_errors(j, W, t_ref, c_ref, M_ref, rows):
    n = M_ref.shape[1]
    cols = pl.ds(j * n, n)
    C = M_ref[:n, :]
    e = errors(dot(W, C, 1, 1), t_ref[rows, cols], c_ref[rows, cols], M_ref[n : n + 1, :])
    return e, C


def row_part_kernel(t_ref, c_ref, M_ref, W_ref, g_ref):
    for rows in row_spans(W_ref.shape[0], 256):
        e, C = half_errors(0, W_ref[rows, :], t_ref, c_ref, M_ref, rows)
        g_ref[rows, :] = dot(e, C, 1, 0)


def row_col_kernel(
    size, halves, after, t_ref, c_ref, M0_ref, M1_ref, W_ref, A_ref, g_ref, Wo_ref, Ao_ref, *h_refs
):
    M_refs = (M0_ref, M1_ref)
    grads = [None] * len(halves)
    for rows in row_spans(W_ref.shape[0], size):
        W = W_ref[rows, :]
        e, C = half_errors(1, W, t_ref, c_ref, M1_ref, rows)
        W, A = adagrad(W, A_ref[rows, :], g_ref[rows, :] + dot(e, C, 1, 0))
        Wo_ref[rows, :] = W
        Ao_ref[rows, :] = A
        after(rows)
        for k, j in enumerate(halves):
            part = dot(W, half_errors(j, W, t_ref, c_ref, M_refs[j], rows)[0], 0, 0)
            grads[k] = part if grads[k] is None else grads[k] + part
    for grad, h_ref in zip(grads, h_refs):
        h_ref[...] = grad.T


def last_kernel(*refs):
    ins, (Wo_hbm, Ao_hbm, h0_ref, h1_ref, W_buf, A_buf, sems) = refs[:7], refs[7:]
    stores = []

    def after(rows):
        pairs = [(W_buf.at[rows], Wo_hbm.at[rows]), (A_buf.at[rows], Ao_hbm.at[rows])]
        stores.extend(fetches(pairs, sems.at[len(stores) // 2]))

    row_col_kernel(512, (0, 1), after, *ins, W_buf, A_buf, h0_ref, h1_ref)
    for copy in stores:
        copy.wait()


def col_kernel(j, t_ref, c_ref, M_ref, W_ref, h_ref):
    grad = None
    for rows in row_spans(W_ref.shape[0], 256):
        W = W_ref[rows, :]
        e, _ = half_errors(j, W, t_ref, c_ref, M_ref, rows)
        part = dot(W, e, 0, 0)
        grad = part if grad is None else grad + part
    h_ref[...] = grad.T


def update_kernel(h_ref, M_ref, B_ref, Mo_ref, Bo_ref):
    n = h_ref.shape[0]
    Mo_ref[:n, :], Bo_ref[...] = adagrad(M_ref[:n, :], B_ref[...], h_ref[...])
    Mo_ref[n:, :] = M_ref[n:, :]


def final_kernel(*refs):
    ins, (Co_ref, Bo_ref) = refs[:-2], refs[-2:]
    n = ins[0].shape[0]
    for j in range(HALVES):
        h_ref, M_ref, B_ref = ins[3 * j : 3 * j + 3]
        rows = pl.ds(j * n, n)
        Co_ref[rows, :], Bo_ref[rows, :] = adagrad(M_ref[:n, :], B_ref[...], h_ref[...])


def call(kernel, operands, spaces, outs, out_spaces, scratch, mib):
    return pl.pallas_call(
        kernel,
        in_specs=[pl.BlockSpec(memory_space=s) for s in spaces],
        out_specs=[pl.BlockSpec(memory_space=s) for s in out_spaces],
        out_shape=[jax.ShapeDtypeStruct(s, f32) for s in outs],
        scratch_shapes=scratch,
        compiler_params=pltpu.CompilerParams(vmem_limit_bytes=mib << 20),
    )(*operands)


def body(tile_counts, row_counts, col_counts, row_factors, row_accum, col_factors, col_accum):
    steps = tile_counts.shape[1]
    n_outer, n_inner = lax.axis_size("outer"), lax.axis_size("inner")

    def move(block, across, by=1):
        route = [
            (o * n_inner + i, (o + across) % n_outer * n_inner + (i + by) % n_inner)
            for o in range(n_outer)
            for i in range(n_inner)
        ]
        return lax.ppermute(block, ("outer", "inner"), route)

    rows = row_counts.reshape(-1, 128)
    cols = col_counts.reshape(1, -1)
    hbm = [tile_counts, rows, cols, row_factors, row_accum, col_factors, col_accum]
    hbm = [pltpu.with_memory_space_constraint(a, H) for a in hbm]
    wide, tall = row_factors.shape, col_factors.shape
    tile = tile_counts.shape[2:]
    half = (tall[0] // HALVES, tall[1])
    message = (half[0] + 8, half[1])
    W, A, t, c, *blocks = call(
        first_kernel, hbm, [H] * 7,
        [wide, wide, tile, tile] + [message] * HALVES + [half] * HALVES, [V] * (4 + 2 * HALVES),
        [V(tile, jnp.int32), V(wide, f32), V(wide, f32), V(rows.shape, jnp.int32),
         V(cols.shape, jnp.int32), DMA((4 + 3 * 2,)), DMA((HALVES,))],
        24,
    )
    M, B = blocks[:HALVES], blocks[HALVES:]

    def update(h, value, total):
        return call(update_kernel, (h, value, total), [V] * 3, [message, half], [V] * 2, [], 4)

    halfway = steps // 2
    early = None
    for step in range(steps):
        h = None
        if step > 0:
            if step == halfway:
                M[0], B[0] = update(M[0], *early)
            part = call(row_part_kernel, (t, c, M[0], W), [V] * 4, [wide], [V], [], 12)[0]
            operands = (t, c, M[0], M[1], W, A, part)
            if step + 1 == steps:
                W, A, *grads = call(
                    last_kernel, operands, [V] * 7, [wide, wide, half, half], [H, H, V, V],
                    [V(wide, f32), V(wide, f32), DMA((2, 2))], 20,
                )
                break
            W, A, h = call(
                functools.partial(row_col_kernel, 256, (0,), lambda rows: None), operands, [V] * 7,
                [wide, wide, half], [V] * 3, [], 16,
            )
        if h is None:
            h = call(functools.partial(col_kernel, 0), (t, c, M[0], W), [V] * 4, [half], [V], [], 12)[0]
        across = int(step + 1 == halfway)
        if across:
            sent = [move(h, across)]
        else:
            value, total = update(h, M[0], B[0])
            sent = [move(value, across)]
        h = call(functools.partial(col_kernel, 1), (t, c, M[1], W), [V] * 4, [half], [V], [], 12)[0]
        last_value, last_total = update(h, M[1], B[1])
        sent.append(move(last_value, across))
        row_tie = lax.optimization_barrier((rows, last_total))[0]
        t, c = call(
            functools.partial(terms_kernel, step + 1), (hbm[0], row_tie), [H, V], [tile, tile], [V] * 2,
            [V(tile, jnp.int32), DMA((4,))], 12,
        )
        M, B = sent, [None, move(last_total, across)]
        if step + 2 == halfway:
            early = [move(value, 1, 2), move(total, 1, 2)]
        elif not across:
            B[0] = move(total, across)
    operands = (grads[0], M[0], B[0], grads[1], M[1], B[1])
    C, B = call(final_kernel, operands, [V] * 6, [tall, tall], [V] * 2, [], 6)
    return W, A, C, B


def solution(mesh):
    both = ("outer", "inner")
    return jax.shard_map(
        body,
        mesh=mesh,
        in_specs=(P(both, None, None, None), P(both), P(both)) + (P(both, None),) * 4,
        out_specs=(P(both, None),) * 4,
        check_vma=False,
    )
```

```python
import functools

import jax
import jax.numpy as jnp
from jax import lax
from jax.experimental import pallas as pl
from jax.experimental.pallas import tpu as pltpu
from jax.sharding import PartitionSpec as P


LOG_TOTAL = 17.0
LEARNING = 0.05
HALVES = 2
FIRST = 256
f32 = jnp.float32
V, H, DMA = pltpu.VMEM, pltpu.HBM, pltpu.SemaphoreType.DMA


def dot(a, b, ca, cb):
    return lax.dot_general(
        a, b, (((ca,), (cb,)), ((), ())), precision=lax.Precision.HIGH, preferred_element_type=f32
    )


def adagrad(value, total, grad):
    total = total + grad * grad
    return value - LEARNING * (grad * lax.rsqrt(total)), total


def fetches(pairs, sems):
    copies = [pltpu.make_async_copy(src, dst, sems.at[i]) for i, (src, dst) in enumerate(pairs)]
    for copy in copies:
        copy.start()
    return copies


def row_spans(n, size):
    return [pl.ds(start, size) for start in range(0, n, size)]


def terms(x, row_logs, first):
    m = jnp.maximum(x.astype(f32), 1.0)
    lanes = row_logs.shape[0]
    logs = [row_logs[:, j : j + 1] for j in range(first, first + x.shape[0] // lanes)]
    target = jnp.log(m) - jnp.concatenate(logs, axis=0)
    return target, jnp.where(x > 0, 0.1 + 0.25 * (m * lax.rsqrt(m)), 0.0)


def errors(z, target, confidence, col_logs):
    gap = (z - target) + col_logs
    return jnp.where(confidence > 0.0, confidence * gap, 0.5 * jnp.tanh(0.5 * gap) + 0.5)


def shifted_row_logs(rows_ref):
    return jnp.log(rows_ref[...].astype(f32)).T - LOG_TOTAL


def terms_kernel(step, x_hbm, rows_ref, t_ref, c_ref, x_buf, sems):
    spans = row_spans(x_buf.shape[0], 256)
    copies = fetches([(x_hbm.at[0, step, rows], x_buf.at[rows]) for rows in spans], sems)
    row_logs = shifted_row_logs(rows_ref)
    for i, rows in enumerate(spans):
        copies[i].wait()
        t_ref[rows, :], c_ref[rows, :] = terms(x_buf[rows, :], row_logs, 2 * i)


def first_kernel(
    x_hbm, rows_hbm, cols_hbm, W_hbm, A_hbm, C_hbm, B_hbm, Wo_ref, Ao_ref, t_ref, c_ref, h_ref, *rest
):
    M_refs, B_refs = rest[:HALVES], rest[HALVES : 2 * HALVES]
    x_buf, W_buf, A_buf, rows_buf, cols_buf, sems, late_sems = rest[2 * HALVES :]
    n, width = B_refs[0].shape
    spans = row_spans(x_buf.shape[0], FIRST)
    pairs = [(cols_hbm, cols_buf), (rows_hbm, rows_buf)]
    pairs += [(C_hbm.at[pl.ds(j * n, n)], M_refs[j].at[pl.ds(0, n)]) for j in range(HALVES)]
    head = len(pairs)
    for rows in spans:
        pairs.append((W_hbm.at[rows], W_buf.at[rows]))
        pairs.append((x_hbm.at[0, 0, rows], x_buf.at[rows]))
        pairs.append((A_hbm.at[rows], A_buf.at[rows]))
    copies = fetches(pairs, sems)
    late = fetches([(B_hbm.at[pl.ds(j * n, n)], B_refs[j]) for j in range(HALVES)], late_sems)
    for copy in copies[:head]:
        copy.wait()
    col_logs = jnp.log(cols_buf[...].astype(f32))
    row_logs = shifted_row_logs(rows_buf)
    for j in range(HALVES):
        M_refs[j][n:, :] = jnp.broadcast_to(col_logs[:, j * n : (j + 1) * n], (8, width))
    C0 = M_refs[0][:n, :]
    C = jnp.concatenate([ref[:n, :] for ref in M_refs], axis=0)
    grad = None
    for i, rows in enumerate(spans):
        for copy in copies[head + 3 * i : head + 3 * i + 3]:
            copy.wait()
        t, c = terms(x_buf[rows, :], row_logs, i * FIRST // row_logs.shape[0])
        t_ref[rows, :] = t[:, n:]
        c_ref[rows, :] = c[:, n:]
        W = W_buf[rows, :]
        g = dot(errors(dot(W, C, 1, 1), t, c, col_logs), C, 1, 0)
        W, Ao_ref[rows, :] = adagrad(W, A_buf[rows, :], g)
        Wo_ref[rows, :] = W
        part = dot(W, errors(dot(W, C0, 1, 1), t[:, :n], c[:, :n], col_logs[:, :n]), 0, 0)
        grad = part if grad is None else grad + part
    h_ref[...] = grad.T
    for copy in late:
        copy.wait()


def half_errors(j, W, t_ref, c_ref, M_ref, rows):
    n = M_ref.shape[1]
    cols = pl.ds(j * n if t_ref.shape[1] > n else 0, n)
    C = M_ref[:n, :]
    e = errors(dot(W, C, 1, 1), t_ref[rows, cols], c_ref[rows, cols], M_ref[n : n + 1, :])
    return e, C


def row_part_kernel(t_ref, c_ref, M_ref, W_ref, g_ref):
    for rows in row_spans(W_ref.shape[0], 256):
        e, C = half_errors(0, W_ref[rows, :], t_ref, c_ref, M_ref, rows)
        g_ref[rows, :] = dot(e, C, 1, 0)


def row_col_kernel(
    size, halves, after, t_ref, c_ref, M0_ref, M1_ref, W_ref, A_ref, g_ref, Wo_ref, Ao_ref, *h_refs
):
    M_refs = (M0_ref, M1_ref)
    grads = [None] * len(halves)
    for rows in row_spans(W_ref.shape[0], size):
        W = W_ref[rows, :]
        e, C = half_errors(1, W, t_ref, c_ref, M1_ref, rows)
        W, A = adagrad(W, A_ref[rows, :], g_ref[rows, :] + dot(e, C, 1, 0))
        Wo_ref[rows, :] = W
        Ao_ref[rows, :] = A
        after(rows)
        for k, j in enumerate(halves):
            part = dot(W, half_errors(j, W, t_ref, c_ref, M_refs[j], rows)[0], 0, 0)
            grads[k] = part if grads[k] is None else grads[k] + part
    for grad, h_ref in zip(grads, h_refs):
        h_ref[...] = grad.T


def last_kernel(*refs):
    ins, (Wo_hbm, Ao_hbm, h0_ref, h1_ref, W_buf, A_buf, sems) = refs[:7], refs[7:]
    stores = []

    def after(rows):
        pairs = [(W_buf.at[rows], Wo_hbm.at[rows]), (A_buf.at[rows], Ao_hbm.at[rows])]
        stores.extend(fetches(pairs, sems.at[len(stores) // 2]))

    row_col_kernel(512, (0, 1), after, *ins, W_buf, A_buf, h0_ref, h1_ref)
    for copy in stores:
        copy.wait()


def col_kernel(j, t_ref, c_ref, M_ref, W_ref, h_ref):
    grad = None
    for rows in row_spans(W_ref.shape[0], 256):
        W = W_ref[rows, :]
        e, _ = half_errors(j, W, t_ref, c_ref, M_ref, rows)
        part = dot(W, e, 0, 0)
        grad = part if grad is None else grad + part
    h_ref[...] = grad.T


def update_kernel(h_ref, M_ref, B_ref, Mo_ref, Bo_ref):
    n = h_ref.shape[0]
    Mo_ref[:n, :], Bo_ref[...] = adagrad(M_ref[:n, :], B_ref[...], h_ref[...])
    Mo_ref[n:, :] = M_ref[n:, :]


def final_kernel(*refs):
    ins, (Co_hbm, Bo_hbm, C_buf, B_buf, sems) = refs[:-5], refs[-5:]
    n = ins[0].shape[0]
    copies = []
    for j in range(HALVES):
        h_ref, M_ref, B_ref = ins[3 * j : 3 * j + 3]
        rows = pl.ds(j * n, n)
        C_buf[rows, :], B_buf[rows, :] = adagrad(M_ref[:n, :], B_ref[...], h_ref[...])
        pairs = [(C_buf.at[rows], Co_hbm.at[rows]), (B_buf.at[rows], Bo_hbm.at[rows])]
        copies += fetches(pairs, sems.at[j])
    for copy in copies:
        copy.wait()


def call(kernel, operands, spaces, outs, out_spaces, scratch, mib):
    return pl.pallas_call(
        kernel,
        in_specs=[pl.BlockSpec(memory_space=s) for s in spaces],
        out_specs=[pl.BlockSpec(memory_space=s) for s in out_spaces],
        out_shape=[jax.ShapeDtypeStruct(s, f32) for s in outs],
        scratch_shapes=scratch,
        compiler_params=pltpu.CompilerParams(vmem_limit_bytes=mib << 20),
    )(*operands)


def body(tile_counts, row_counts, col_counts, row_factors, row_accum, col_factors, col_accum):
    steps = tile_counts.shape[1]
    n_outer, n_inner = lax.axis_size("outer"), lax.axis_size("inner")

    def move(block, across):
        route = [
            (o * n_inner + i, (o + across) % n_outer * n_inner + (i + 1) % n_inner)
            for o in range(n_outer)
            for i in range(n_inner)
        ]
        return lax.ppermute(block, ("outer", "inner"), route)

    rows = row_counts.reshape(-1, 128)
    cols = col_counts.reshape(1, -1)
    hbm = [tile_counts, rows, cols, row_factors, row_accum, col_factors, col_accum]
    hbm = [pltpu.with_memory_space_constraint(a, H) for a in hbm]
    wide, tall = row_factors.shape, col_factors.shape
    tile = tile_counts.shape[2:]
    half = (tall[0] // HALVES, tall[1])
    message = (half[0] + 8, half[1])
    part = (tile[0], half[0])
    W, A, t, c, h, *blocks = call(
        first_kernel, hbm, [H] * 7,
        [wide, wide, part, part, half] + [message] * HALVES + [half] * HALVES, [V] * (5 + 2 * HALVES),
        [V(tile, jnp.int32), V(wide, f32), V(wide, f32), V(rows.shape, jnp.int32),
         V(cols.shape, jnp.int32), DMA((4 + 3 * (tile[0] // FIRST),)), DMA((HALVES,))],
        24,
    )
    M, B = blocks[:HALVES], blocks[HALVES:]

    def update(h, value, total):
        return call(update_kernel, (h, value, total), [V] * 3, [message, half], [V] * 2, [], 4)

    def next_terms(step, tie):
        row_tie = lax.optimization_barrier((rows, tie))[0]
        return call(
            functools.partial(terms_kernel, step + 1), (hbm[0], row_tie), [H, V], [tile, tile], [V] * 2,
            [V(tile, jnp.int32), DMA((4,))], 12,
        )

    halfway = steps // 2
    for step in range(steps):
        h1 = None
        if step > 0:
            g = call(row_part_kernel, (t, c, M[0], W), [V] * 4, [wide], [V], [], 12)[0]
            operands = (t, c, M[0], M[1], W, A, g)
            if step + 1 == steps:
                W, A, h, h1 = call(
                    last_kernel, operands, [V] * 7, [wide, wide, half, half], [H, H, V, V],
                    [V(wide, f32), V(wide, f32), DMA((2, 2))], 20,
                )
                break
            if step == halfway:
                W, A, h, h1 = call(
                    functools.partial(row_col_kernel, 512, (0, 1), lambda rows: None), operands, [V] * 7,
                    [wide, wide, half, half], [V] * 4, [], 20,
                )
            else:
                W, A, h = call(
                    functools.partial(row_col_kernel, 256, (0,), lambda rows: None), operands, [V] * 7,
                    [wide, wide, half], [V] * 3, [], 16,
                )
        across = int(step + 1 == halfway)
        value, total = update(h, M[0], B[0])
        sent = [move(value, across)]
        if h1 is None:
            h1 = call(functools.partial(col_kernel, 1), (t, c, M[1], W), [V] * 4, [half], [V], [], 12)[0]
        else:
            t, c = next_terms(step, total)
            h1 = lax.optimization_barrier((h1, t))[0]
        last_value, last_total = update(h1, M[1], B[1])
        if step != halfway:
            t, c = next_terms(step, last_total)
        sent.append(move(last_value, across))
        M, B = sent, [move(total, across), move(last_total, across)]
    operands = (h, M[0], B[0], h1, M[1], B[1])
    C, B = call(
        final_kernel, operands, [V] * 6, [tall, tall], [H] * 2,
        [V(tall, f32), V(tall, f32), DMA((HALVES, 2))], 6,
    )
    return W, A, C, B


def solution(mesh):
    both = ("outer", "inner")
    return jax.shard_map(
        body,
        mesh=mesh,
        in_specs=(P(both, None, None, None), P(both), P(both)) + (P(both, None),) * 4,
        out_specs=(P(both, None),) * 4,
        check_vma=False,
    )
```

```python
import functools

import jax
import jax.numpy as jnp
from jax import lax
from jax.experimental import pallas as pl
from jax.experimental.pallas import tpu as pltpu
from jax.sharding import PartitionSpec as P


LOG_TOTAL = 17.0
LEARNING = 0.05
HALVES = 2
f32 = jnp.float32
V, H, DMA = pltpu.VMEM, pltpu.HBM, pltpu.SemaphoreType.DMA


def dot(a, b, ca, cb):
    return lax.dot_general(
        a, b, (((ca,), (cb,)), ((), ())), precision=lax.Precision.HIGH, preferred_element_type=f32
    )


def adagrad(value, total, grad):
    total = total + grad * grad
    return value - LEARNING * (grad * lax.rsqrt(total)), total


def fetches(pairs, sems):
    copies = [pltpu.make_async_copy(src, dst, sems.at[i]) for i, (src, dst) in enumerate(pairs)]
    for copy in copies:
        copy.start()
    return copies


def row_spans(n, size):
    return [pl.ds(start, size) for start in range(0, n, size)]


def put_terms(x, row_logs, first, t_ref, c_ref, rows):
    m = jnp.maximum(x.astype(f32), 1.0)
    lanes = row_logs.shape[0]
    logs = [row_logs[:, j : j + 1] for j in range(first, first + x.shape[0] // lanes)]
    t_ref[rows, :] = jnp.log(m) - jnp.concatenate(logs, axis=0)
    c_ref[rows, :] = jnp.where(x > 0, 0.1 + 0.25 * (m * lax.rsqrt(m)), 0.0)


def errors(z, target, confidence, col_logs):
    gap = (z - target) + col_logs
    return jnp.where(confidence > 0.0, confidence * gap, 0.5 * jnp.tanh(0.5 * gap) + 0.5)


def shifted_row_logs(rows_ref):
    return jnp.log(rows_ref[...].astype(f32)).T - LOG_TOTAL


def terms_kernel(step, x_hbm, rows_ref, t_ref, c_ref, x_buf, sems):
    spans = row_spans(x_buf.shape[0], 256)
    copies = fetches([(x_hbm.at[0, step, rows], x_buf.at[rows]) for rows in spans], sems)
    row_logs = shifted_row_logs(rows_ref)
    for i, rows in enumerate(spans):
        copies[i].wait()
        put_terms(x_buf[rows, :], row_logs, 2 * i, t_ref, c_ref, rows)


def first_kernel(
    x_hbm, rows_hbm, cols_hbm, W_hbm, A_hbm, C_hbm, B_hbm,
    Wo_ref, Ao_ref, t_ref, c_ref, *rest,
):
    M_refs, B_refs = rest[:HALVES], rest[HALVES : 2 * HALVES]
    x_buf, W_buf, A_buf, rows_buf, cols_buf, sems, out_sems = rest[2 * HALVES :]
    n, width = B_refs[0].shape
    spans = row_spans(x_buf.shape[0], 512)
    pairs = [(cols_hbm, cols_buf), (rows_hbm, rows_buf)]
    pairs += [(C_hbm.at[pl.ds(j * n, n)], M_refs[j].at[pl.ds(0, n)]) for j in range(HALVES)]
    head = len(pairs)
    for rows in spans:
        pairs.append((W_hbm.at[rows], W_buf.at[rows]))
        pairs.append((x_hbm.at[0, 0, rows], x_buf.at[rows]))
        pairs.append((A_hbm.at[rows], A_buf.at[rows]))
    copies = fetches(pairs, sems)
    late = fetches([(B_hbm.at[pl.ds(j * n, n)], B_refs[j]) for j in range(HALVES)], out_sems)
    for copy in copies[:head]:
        copy.wait()
    col_logs = jnp.log(cols_buf[...].astype(f32))
    row_logs = shifted_row_logs(rows_buf)
    for j in range(HALVES):
        M_refs[j][n:, :] = jnp.broadcast_to(col_logs[:, j * n : (j + 1) * n], (8, width))
    C = jnp.concatenate([ref[:n, :] for ref in M_refs], axis=0)
    for i, rows in enumerate(spans):
        for copy in copies[head + 3 * i : head + 3 * i + 3]:
            copy.wait()
        put_terms(x_buf[rows, :], row_logs, 4 * i, t_ref, c_ref, rows)
        W = W_buf[rows, :]
        e = errors(dot(W, C, 1, 1), t_ref[rows, :], c_ref[rows, :], col_logs)
        Wo_ref[rows, :], Ao_ref[rows, :] = adagrad(W, A_buf[rows, :], dot(e, C, 1, 0))
    for copy in late:
        copy.wait()


def half_errors(j, W, t_ref, c_ref, M_ref, rows):
    n = M_ref.shape[1]
    cols = pl.ds(j * n, n)
    C = M_ref[:n, :]
    e = errors(dot(W, C, 1, 1), t_ref[rows, cols], c_ref[rows, cols], M_ref[n : n + 1, :])
    return e, C


def row_part_kernel(t_ref, c_ref, M_ref, W_ref, g_ref):
    for rows in row_spans(W_ref.shape[0], 256):
        e, C = half_errors(0, W_ref[rows, :], t_ref, c_ref, M_ref, rows)
        g_ref[rows, :] = dot(e, C, 1, 0)


def row_col_kernel(
    size, halves, after, t_ref, c_ref, M0_ref, M1_ref, W_ref, A_ref, g_ref, Wo_ref, Ao_ref, *h_refs
):
    M_refs = (M0_ref, M1_ref)
    grads = [None] * len(halves)
    for rows in row_spans(W_ref.shape[0], size):
        W = W_ref[rows, :]
        e, C = half_errors(1, W, t_ref, c_ref, M1_ref, rows)
        W, A = adagrad(W, A_ref[rows, :], g_ref[rows, :] + dot(e, C, 1, 0))
        Wo_ref[rows, :] = W
        Ao_ref[rows, :] = A
        after(rows)
        for k, j in enumerate(halves):
            part = dot(W, half_errors(j, W, t_ref, c_ref, M_refs[j], rows)[0], 0, 0)
            grads[k] = part if grads[k] is None else grads[k] + part
    for grad, h_ref in zip(grads, h_refs):
        h_ref[...] = grad.T


def last_kernel(*refs):
    ins, (Wo_hbm, Ao_hbm, h0_ref, h1_ref, W_buf, A_buf, sems) = refs[:7], refs[7:]
    stores = []

    def after(rows):
        pairs = [(W_buf.at[rows], Wo_hbm.at[rows]), (A_buf.at[rows], Ao_hbm.at[rows])]
        stores.extend(fetches(pairs, sems.at[len(stores) // 2]))

    row_col_kernel(512, (0, 1), after, *ins, W_buf, A_buf, h0_ref, h1_ref)
    for copy in stores:
        copy.wait()


def col_kernel(j, t_ref, c_ref, M_ref, W_ref, h_ref):
    grad = None
    for rows in row_spans(W_ref.shape[0], 256):
        W = W_ref[rows, :]
        part = dot(half_errors(j, W, t_ref, c_ref, M_ref, rows)[0], W, 0, 0)
        grad = part if grad is None else grad + part
    h_ref[...] = grad


def join_kernel(a_ref, b_ref, o_ref):
    o_ref[...] = a_ref[...] + b_ref[...]


def update_kernel(h_ref, M_ref, B_ref, Mo_ref, Bo_ref):
    n = h_ref.shape[0]
    Mo_ref[:n, :], Bo_ref[...] = adagrad(M_ref[:n, :], B_ref[...], h_ref[...])
    Mo_ref[n:, :] = M_ref[n:, :]


def final_kernel(*refs):
    ins, (Co_ref, Bo_ref) = refs[:-2], refs[-2:]
    n = ins[0].shape[0]
    for j in range(HALVES):
        h_ref, M_ref, B_ref = ins[3 * j : 3 * j + 3]
        rows = pl.ds(j * n, n)
        Co_ref[rows, :], Bo_ref[rows, :] = adagrad(M_ref[:n, :], B_ref[...], h_ref[...])


def call(kernel, operands, spaces, outs, out_spaces, scratch, mib):
    return pl.pallas_call(
        kernel,
        in_specs=[pl.BlockSpec(memory_space=s) for s in spaces],
        out_specs=[pl.BlockSpec(memory_space=s) for s in out_spaces],
        out_shape=[jax.ShapeDtypeStruct(s, f32) for s in outs],
        scratch_shapes=scratch,
        compiler_params=pltpu.CompilerParams(vmem_limit_bytes=mib << 20),
    )(*operands)


def body(tile_counts, row_counts, col_counts, row_factors, row_accum, col_factors, col_accum):
    steps = tile_counts.shape[1]
    n_outer, n_inner = lax.axis_size("outer"), lax.axis_size("inner")

    def move(block, across, senders=(0, 1)):
        route = [
            (o * n_inner + i, (o + across) % n_outer * n_inner + (i + 1) % n_inner)
            for o in range(n_outer)
            for i in range(n_inner)
            if i % 2 in senders
        ]
        return lax.ppermute(block, ("outer", "inner"), route)

    def join(pair):
        shape = pair[0].shape
        return call(join_kernel, pair, [V] * 2, [shape], [V], [], 4)[0]

    rows = row_counts.reshape(-1, 128)
    cols = col_counts.reshape(1, -1)
    hbm = [tile_counts, rows, cols, row_factors, row_accum, col_factors, col_accum]
    hbm = [pltpu.with_memory_space_constraint(a, H) for a in hbm]
    wide, tall = row_factors.shape, col_factors.shape
    tile = tile_counts.shape[2:]
    half = (tall[0] // HALVES, tall[1])
    message = (half[0] + 8, half[1])
    W, A, t, c, *blocks = call(
        first_kernel, hbm, [H] * 7,
        [wide, wide, tile, tile] + [message] * HALVES + [half] * HALVES, [V] * (4 + 2 * HALVES),
        [V(tile, jnp.int32), V(wide, f32), V(wide, f32), V(rows.shape, jnp.int32),
         V(cols.shape, jnp.int32), DMA((4 + 3 * 2,)), DMA((HALVES,))],
        24,
    )
    M, B = blocks[:HALVES], blocks[HALVES:]

    def update(h, value, total):
        return call(update_kernel, (h, value, total), [V] * 3, [message, half], [V] * 2, [], 4)

    def next_terms(step, tie):
        row_tie = lax.optimization_barrier((rows, tie))[0]
        return call(
            functools.partial(terms_kernel, step + 1), (hbm[0], row_tie), [H, V], [tile, tile], [V] * 2,
            [V(tile, jnp.int32), DMA((4,))], 12,
        )

    halfway = steps // 2
    for step in range(steps):
        h = None
        if step > 0:
            g = call(row_part_kernel, (t, c, M[0], W), [V] * 4, [wide], [V], [], 12)[0]
            operands = (t, c, M[0], M[1], W, A, g)
            if step + 1 == steps:
                W, A, *grads = call(
                    last_kernel, operands, [V] * 7, [wide, wide, half, half], [H, H, V, V],
                    [V(wide, f32), V(wide, f32), DMA((2, 2))], 20,
                )
                break
            if step == halfway:
                W, A, *grads = call(
                    functools.partial(row_col_kernel, 512, (0, 1), lambda rows: None), operands, [V] * 7,
                    [wide, wide, half, half], [V] * 4, [], 20,
                )
            else:
                W, A, h = call(
                    functools.partial(row_col_kernel, 256, (0,), lambda rows: None), operands, [V] * 7,
                    [wide, wide, half], [V] * 3, [], 16,
                )
        if step == halfway:
            odd = [update(grads[j], M[j], B[j][0])[0] for j in range(HALVES)]
            to_even = [move(odd[j], 0, (1,)) for j in range(HALVES)]
            tied = lax.optimization_barrier((*grads, *odd))[:HALVES]
            both = [update(tied[j], M[j], join(B[j])) for j in range(HALVES)]
            to_odd = [move(both[j][0], 0, (0,)) for j in range(HALVES)]
            t, c = next_terms(step, both[1][1])
            M = [join(pair) for pair in zip(to_even, to_odd)]
            B = [move(both[j][1], 0) for j in range(HALVES)]
            continue
        across = int(step + 1 == halfway)
        sent, sums = [], []
        for j in range(HALVES):
            if h is None or j > 0:
                operands = (t, c, M[j], W)
                h = call(functools.partial(col_kernel, j), operands, [V] * 4, [half], [V], [], 12)[0]
            value, total = update(h, M[j], B[j])
            sent.append(move(value, across))
            sums.append(total)
        t, c = next_terms(step, sums[-1])
        M = sent
        if across:
            B = [(move(total, across, (0,)), move(total, across, (1,))) for total in sums]
        else:
            B = [move(total, across) for total in sums]
    operands = (grads[0], M[0], B[0], grads[1], M[1], B[1])
    C, B = call(final_kernel, operands, [V] * 6, [tall, tall], [V] * 2, [], 6)
    return W, A, C, B


def solution(mesh):
    both = ("outer", "inner")
    return jax.shard_map(
        body,
        mesh=mesh,
        in_specs=(P(both, None, None, None), P(both), P(both)) + (P(both, None),) * 4,
        out_specs=(P(both, None),) * 4,
        check_vma=False,
    )
```

```python
import functools

import jax
import jax.numpy as jnp
from jax import lax
from jax.experimental import pallas as pl
from jax.experimental.pallas import tpu as pltpu
from jax.sharding import PartitionSpec as P


LOG_TOTAL = 17.0
LEARNING = 0.05
HALVES = 2
f32 = jnp.float32
V, H, DMA = pltpu.VMEM, pltpu.HBM, pltpu.SemaphoreType.DMA


def dot(a, b, ca, cb):
    return lax.dot_general(
        a, b, (((ca,), (cb,)), ((), ())), precision=lax.Precision.HIGH, preferred_element_type=f32
    )


def adagrad(value, total, grad):
    total = total + grad * grad
    return value - LEARNING * (grad * lax.rsqrt(total)), total


def fetches(pairs, sems):
    copies = [pltpu.make_async_copy(src, dst, sems.at[i]) for i, (src, dst) in enumerate(pairs)]
    for copy in copies:
        copy.start()
    return copies


def row_spans(n, size):
    return [pl.ds(start, size) for start in range(0, n, size)]


def put_terms(x, row_logs, first, t_ref, c_ref, rows):
    m = jnp.maximum(x.astype(f32), 1.0)
    lanes = row_logs.shape[0]
    logs = [row_logs[:, j : j + 1] for j in range(first, first + x.shape[0] // lanes)]
    t_ref[rows, :] = jnp.log(m) - jnp.concatenate(logs, axis=0)
    c_ref[rows, :] = jnp.where(x > 0, 0.1 + 0.25 * (m * lax.rsqrt(m)), 0.0)


def errors(z, target, confidence, col_logs):
    gap = (z - target) + col_logs
    return jnp.where(confidence > 0.0, confidence * gap, 0.5 * jnp.tanh(0.5 * gap) + 0.5)


def shifted_row_logs(rows_ref):
    return jnp.log(rows_ref[...].astype(f32)).T - LOG_TOTAL


def terms_kernel(step, x_hbm, rows_ref, t_ref, c_ref, x_buf, sems):
    spans = row_spans(x_buf.shape[0], 256)
    copies = fetches([(x_hbm.at[0, step, rows], x_buf.at[rows]) for rows in spans], sems)
    row_logs = shifted_row_logs(rows_ref)
    for i, rows in enumerate(spans):
        copies[i].wait()
        put_terms(x_buf[rows, :], row_logs, 2 * i, t_ref, c_ref, rows)


def first_kernel(
    x_hbm, rows_hbm, cols_hbm, W_hbm, A_hbm, C_hbm, B_hbm,
    Wo_ref, Ao_ref, t_ref, c_ref, *rest,
):
    M_refs, B_refs = rest[:HALVES], rest[HALVES : 2 * HALVES]
    x_buf, W_buf, A_buf, rows_buf, cols_buf, sems, out_sems = rest[2 * HALVES :]
    n, width = B_refs[0].shape
    spans = row_spans(x_buf.shape[0], 512)
    pairs = [(cols_hbm, cols_buf), (rows_hbm, rows_buf)]
    pairs += [(C_hbm.at[pl.ds(j * n, n)], M_refs[j].at[pl.ds(0, n)]) for j in range(HALVES)]
    head = len(pairs)
    for rows in spans:
        pairs.append((W_hbm.at[rows], W_buf.at[rows]))
        pairs.append((x_hbm.at[0, 0, rows], x_buf.at[rows]))
        pairs.append((A_hbm.at[rows], A_buf.at[rows]))
    copies = fetches(pairs, sems)
    late = fetches([(B_hbm.at[pl.ds(j * n, n)], B_refs[j]) for j in range(HALVES)], out_sems)
    for copy in copies[:head]:
        copy.wait()
    col_logs = jnp.log(cols_buf[...].astype(f32))
    row_logs = shifted_row_logs(rows_buf)
    for j in range(HALVES):
        M_refs[j][n:, :] = jnp.broadcast_to(col_logs[:, j * n : (j + 1) * n], (8, width))
    C = jnp.concatenate([ref[:n, :] for ref in M_refs], axis=0)
    for i, rows in enumerate(spans):
        for copy in copies[head + 3 * i : head + 3 * i + 3]:
            copy.wait()
        put_terms(x_buf[rows, :], row_logs, 4 * i, t_ref, c_ref, rows)
        W = W_buf[rows, :]
        e = errors(dot(W, C, 1, 1), t_ref[rows, :], c_ref[rows, :], col_logs)
        Wo_ref[rows, :], Ao_ref[rows, :] = adagrad(W, A_buf[rows, :], dot(e, C, 1, 0))
    for copy in late:
        copy.wait()


def half_errors(j, W, t_ref, c_ref, M_ref, rows):
    n = M_ref.shape[1]
    cols = pl.ds(j * n, n)
    C = M_ref[:n, :]
    e = errors(dot(W, C, 1, 1), t_ref[rows, cols], c_ref[rows, cols], M_ref[n : n + 1, :])
    return e, C


def row_part_kernel(t_ref, c_ref, M_ref, W_ref, g_ref):
    for rows in row_spans(W_ref.shape[0], 256):
        e, C = half_errors(0, W_ref[rows, :], t_ref, c_ref, M_ref, rows)
        g_ref[rows, :] = dot(e, C, 1, 0)


def row_col_kernel(
    size, halves, after, t_ref, c_ref, M0_ref, M1_ref, W_ref, A_ref, g_ref, Wo_ref, Ao_ref, *h_refs
):
    M_refs = (M0_ref, M1_ref)
    grads = [None] * len(halves)
    for rows in row_spans(W_ref.shape[0], size):
        W = W_ref[rows, :]
        e, C = half_errors(1, W, t_ref, c_ref, M1_ref, rows)
        W, A = adagrad(W, A_ref[rows, :], g_ref[rows, :] + dot(e, C, 1, 0))
        Wo_ref[rows, :] = W
        Ao_ref[rows, :] = A
        after(rows)
        for k, j in enumerate(halves):
            part = dot(W, half_errors(j, W, t_ref, c_ref, M_refs[j], rows)[0], 0, 0)
            grads[k] = part if grads[k] is None else grads[k] + part
    for grad, h_ref in zip(grads, h_refs):
        h_ref[...] = grad.T


def last_kernel(*refs):
    ins, (Wo_hbm, Ao_hbm, h0_ref, h1_ref, W_buf, A_buf, sems) = refs[:7], refs[7:]
    stores = []

    def after(rows):
        pairs = [(W_buf.at[rows], Wo_hbm.at[rows]), (A_buf.at[rows], Ao_hbm.at[rows])]
        stores.extend(fetches(pairs, sems.at[len(stores) // 2]))

    row_col_kernel(512, (0, 1), after, *ins, W_buf, A_buf, h0_ref, h1_ref)
    for copy in stores:
        copy.wait()


def col_kernel(j, t_ref, c_ref, M_ref, W_ref, h_ref):
    grad = None
    for rows in row_spans(W_ref.shape[0], 256):
        W = W_ref[rows, :]
        part = dot(half_errors(j, W, t_ref, c_ref, M_ref, rows)[0], W, 0, 0)
        grad = part if grad is None else grad + part
    h_ref[...] = grad


def update_kernel(h_ref, M_ref, B_ref, Mo_ref, Bo_ref):
    n = h_ref.shape[0]
    Mo_ref[:n, :], Bo_ref[...] = adagrad(M_ref[:n, :], B_ref[...], h_ref[...])
    Mo_ref[n:, :] = M_ref[n:, :]


def final_kernel(*refs):
    ins, (Co_ref, Bo_ref) = refs[:-2], refs[-2:]
    n = ins[0].shape[0]
    for j in range(HALVES):
        h_ref, M_ref, B_ref = ins[3 * j : 3 * j + 3]
        rows = pl.ds(j * n, n)
        Co_ref[rows, :], Bo_ref[rows, :] = adagrad(M_ref[:n, :], B_ref[...], h_ref[...])


def call(kernel, operands, spaces, outs, out_spaces, scratch, mib):
    return pl.pallas_call(
        kernel,
        in_specs=[pl.BlockSpec(memory_space=s) for s in spaces],
        out_specs=[pl.BlockSpec(memory_space=s) for s in out_spaces],
        out_shape=[jax.ShapeDtypeStruct(s, f32) for s in outs],
        scratch_shapes=scratch,
        compiler_params=pltpu.CompilerParams(vmem_limit_bytes=mib << 20),
    )(*operands)


def body(tile_counts, row_counts, col_counts, row_factors, row_accum, col_factors, col_accum):
    steps = tile_counts.shape[1]
    n_outer, n_inner = lax.axis_size("outer"), lax.axis_size("inner")

    def move(block, across):
        route = [
            (o * n_inner + i, (o + across) % n_outer * n_inner + (i + 1) % n_inner)
            for o in range(n_outer)
            for i in range(n_inner)
        ]
        return lax.ppermute(block, ("outer", "inner"), route)

    rows = row_counts.reshape(-1, 128)
    cols = col_counts.reshape(1, -1)
    hbm = [tile_counts, rows, cols, row_factors, row_accum, col_factors, col_accum]
    hbm = [pltpu.with_memory_space_constraint(a, H) for a in hbm]
    wide, tall = row_factors.shape, col_factors.shape
    tile = tile_counts.shape[2:]
    half = (tall[0] // HALVES, tall[1])
    message = (half[0] + 8, half[1])
    W, A, t, c, *blocks = call(
        first_kernel, hbm, [H] * 7,
        [wide, wide, tile, tile] + [message] * HALVES + [half] * HALVES, [V] * (4 + 2 * HALVES),
        [V(tile, jnp.int32), V(wide, f32), V(wide, f32), V(rows.shape, jnp.int32),
         V(cols.shape, jnp.int32), DMA((4 + 3 * 2,)), DMA((HALVES,))],
        24,
    )
    M, B = blocks[:HALVES], blocks[HALVES:]
    for step in range(steps):
        grads = []
        if step > 0:
            g = call(row_part_kernel, (t, c, M[0], W), [V] * 4, [wide], [V], [], 12)[0]
            operands = (t, c, M[0], M[1], W, A, g)
            if step + 1 == steps:
                W, A, *grads = call(
                    last_kernel, operands, [V] * 7, [wide, wide, half, half], [H, H, V, V],
                    [V(wide, f32), V(wide, f32), DMA((2, 2))], 20,
                )
                break
            size, halves = (512, (0, 1)) if step == steps // 2 else (256, (0,))
            W, A, *grads = call(
                functools.partial(row_col_kernel, size, halves, lambda rows: None), operands, [V] * 7,
                [wide, wide] + [half] * len(halves), [V] * (2 + len(halves)), [], 20,
            )
        across = int(step + 1 == steps // 2)
        sent, sums = [], []
        for j in range(HALVES):
            if j == len(grads):
                operands = (t, c, M[j], W)
                grads += call(functools.partial(col_kernel, j), operands, [V] * 4, [half], [V], [], 12)
            value, total = call(update_kernel, (grads[j], M[j], B[j]), [V] * 3, [message, half], [V] * 2, [], 4)
            sent.append(move(value, across))
            sums.append(total)
        row_tie = lax.optimization_barrier((rows, *sums))[0]
        t, c = call(
            functools.partial(terms_kernel, step + 1), (hbm[0], row_tie), [H, V], [tile, tile], [V] * 2,
            [V(tile, jnp.int32), DMA((4,))], 12,
        )
        M, B = sent, [move(total, across) for total in sums]
    operands = (grads[0], M[0], B[0], grads[1], M[1], B[1])
    C, B = call(final_kernel, operands, [V] * 6, [tall, tall], [V] * 2, [], 6)
    return W, A, C, B


def solution(mesh):
    both = ("outer", "inner")
    return jax.shard_map(
        body,
        mesh=mesh,
        in_specs=(P(both, None, None, None), P(both), P(both)) + (P(both, None),) * 4,
        out_specs=(P(both, None),) * 4,
        check_vma=False,
    )
```

```python
import functools

import jax
import jax.numpy as jnp
from jax import lax
from jax.experimental import pallas as pl
from jax.experimental.pallas import tpu as pltpu
from jax.sharding import PartitionSpec as P


LOG_TOTAL = 17.0
LEARNING = 0.05
HALVES = 2
f32 = jnp.float32
V, H, DMA = pltpu.VMEM, pltpu.HBM, pltpu.SemaphoreType.DMA


def dot(a, b, ca, cb):
    return lax.dot_general(
        a, b, (((ca,), (cb,)), ((), ())), precision=lax.Precision.HIGH, preferred_element_type=f32
    )


def adagrad(value, total, grad):
    total = total + grad * grad
    return value - LEARNING * (grad * lax.rsqrt(total)), total


def fetches(pairs, sems):
    copies = [pltpu.make_async_copy(src, dst, sems.at[i]) for i, (src, dst) in enumerate(pairs)]
    for copy in copies:
        copy.start()
    return copies


def row_spans(n, size):
    return [pl.ds(start, size) for start in range(0, n, size)]


def put_terms(x, row_logs, first, t_ref, c_ref, rows):
    m = jnp.maximum(x.astype(f32), 1.0)
    lanes = row_logs.shape[0]
    logs = [row_logs[:, j : j + 1] for j in range(first, first + x.shape[0] // lanes)]
    t_ref[rows, :] = jnp.log(m) - jnp.concatenate(logs, axis=0)
    c_ref[rows, :] = jnp.where(x > 0, 0.1 + 0.25 * (m * lax.rsqrt(m)), 0.0)


def errors(z, target, confidence, col_logs):
    gap = (z - target) + col_logs
    return jnp.where(confidence > 0.0, confidence * gap, 0.5 * jnp.tanh(0.5 * gap) + 0.5)


def shifted_row_logs(rows_ref):
    return jnp.log(rows_ref[...].astype(f32)).T - LOG_TOTAL


def terms_kernel(step, x_hbm, rows_ref, t_ref, c_ref, x_buf, sems):
    spans = row_spans(x_buf.shape[0], 256)
    copies = fetches([(x_hbm.at[0, step, rows], x_buf.at[rows]) for rows in spans], sems)
    row_logs = shifted_row_logs(rows_ref)
    for i, rows in enumerate(spans):
        copies[i].wait()
        put_terms(x_buf[rows, :], row_logs, 2 * i, t_ref, c_ref, rows)


def first_kernel(
    x_hbm, rows_hbm, cols_hbm, W_hbm, A_hbm, C_hbm, B_hbm, Wo_ref, Ao_ref, t_ref, c_ref, h_ref, *rest
):
    M_refs, B_refs = rest[:HALVES], rest[HALVES : 2 * HALVES]
    x_buf, W_buf, A_buf, rows_buf, cols_buf, sems, late_sems = rest[2 * HALVES :]
    n, width = B_refs[0].shape
    quarters, spans = row_spans(x_buf.shape[0], 256), row_spans(x_buf.shape[0], 512)
    pairs = [(cols_hbm, cols_buf), (rows_hbm, rows_buf)]
    pairs += [(C_hbm.at[pl.ds(j * n, n)], M_refs[j].at[pl.ds(0, n)]) for j in range(HALVES)]
    head = len(pairs)
    pairs += [(x_hbm.at[0, 0, rows], x_buf.at[rows]) for rows in quarters]
    body = len(pairs)
    for rows in spans:
        pairs.append((W_hbm.at[rows], W_buf.at[rows]))
        pairs.append((A_hbm.at[rows], A_buf.at[rows]))
    copies = fetches(pairs, sems)
    late = fetches([(B_hbm.at[pl.ds(j * n, n)], B_refs[j]) for j in range(HALVES)], late_sems)
    for copy in copies[:2]:
        copy.wait()
    col_logs = jnp.log(cols_buf[...].astype(f32))
    row_logs = shifted_row_logs(rows_buf)
    for i, rows in enumerate(quarters):
        copies[head + i].wait()
        put_terms(x_buf[rows, :], row_logs, 2 * i, t_ref, c_ref, rows)
    for copy in copies[2:head]:
        copy.wait()
    for j in range(HALVES):
        M_refs[j][n:, :] = jnp.broadcast_to(col_logs[:, j * n : (j + 1) * n], (8, width))
    C = jnp.concatenate([ref[:n, :] for ref in M_refs], axis=0)
    for i, rows in enumerate(spans):
        for copy in copies[body + 2 * i : body + 2 * i + 2]:
            copy.wait()
        W = W_buf[rows, :]
        e = errors(dot(W, C, 1, 1), t_ref[rows, :], c_ref[rows, :], col_logs)
        Wo_ref[rows, :], Ao_ref[rows, :] = adagrad(W, A_buf[rows, :], dot(e, C, 1, 0))
    h_ref[...] = col_gradient((0,), t_ref, c_ref, M_refs[:1], Wo_ref)
    for copy in late:
        copy.wait()


def col_gradient(halves, t_ref, c_ref, M_refs, W_ref):
    n = M_refs[0].shape[1]
    cols = pl.ds(halves[0] * n, len(halves) * n)
    C = jnp.concatenate([ref[:n, :] for ref in M_refs], axis=0)
    col_logs = jnp.concatenate([ref[n : n + 1, :] for ref in M_refs], axis=1)
    grad = None
    for rows in row_spans(W_ref.shape[0], 256):
        W = W_ref[rows, :]
        part = dot(errors(dot(W, C, 1, 1), t_ref[rows, cols], c_ref[rows, cols], col_logs), W, 0, 0)
        grad = part if grad is None else grad + part
    return grad


def half_errors(j, W, t_ref, c_ref, M_ref, rows):
    n = M_ref.shape[1]
    cols = pl.ds(j * n, n)
    C = M_ref[:n, :]
    e = errors(dot(W, C, 1, 1), t_ref[rows, cols], c_ref[rows, cols], M_ref[n : n + 1, :])
    return e, C


def row_part_kernel(t_ref, c_ref, M_ref, W_ref, g_ref):
    for rows in row_spans(W_ref.shape[0], 256):
        e, C = half_errors(0, W_ref[rows, :], t_ref, c_ref, M_ref, rows)
        g_ref[rows, :] = dot(e, C, 1, 0)


def row_col_kernel(
    size, halves, after, t_ref, c_ref, M0_ref, M1_ref, W_ref, A_ref, g_ref, Wo_ref, Ao_ref, *h_refs
):
    for rows in row_spans(W_ref.shape[0], size):
        W = W_ref[rows, :]
        e, C = half_errors(1, W, t_ref, c_ref, M1_ref, rows)
        Wo_ref[rows, :], Ao_ref[rows, :] = adagrad(W, A_ref[rows, :], g_ref[rows, :] + dot(e, C, 1, 0))
        after(rows)
    grad = col_gradient(halves, t_ref, c_ref, (M0_ref, M1_ref)[: len(halves)], Wo_ref)
    for j, h_ref in enumerate(h_refs):
        n = h_ref.shape[0]
        h_ref[...] = grad[j * n : (j + 1) * n, :]


def last_kernel(*refs):
    ins, (Wo_hbm, Ao_hbm, h0_ref, h1_ref, W_buf, A_buf, sems) = refs[:7], refs[7:]
    stores = []

    def after(rows):
        pairs = [(W_buf.at[rows], Wo_hbm.at[rows]), (A_buf.at[rows], Ao_hbm.at[rows])]
        stores.extend(fetches(pairs, sems.at[len(stores) // 2]))

    row_col_kernel(512, (0, 1), after, *ins, W_buf, A_buf, h0_ref, h1_ref)
    for copy in stores:
        copy.wait()


def col_kernel(j, t_ref, c_ref, M_ref, W_ref, h_ref):
    h_ref[...] = col_gradient((j,), t_ref, c_ref, (M_ref,), W_ref)


def update_kernel(h_ref, M_ref, B_ref, Mo_ref, Bo_ref):
    n = h_ref.shape[0]
    Mo_ref[:n, :], Bo_ref[...] = adagrad(M_ref[:n, :], B_ref[...], h_ref[...])
    Mo_ref[n:, :] = M_ref[n:, :]


def final_kernel(*refs):
    ins, (Co_ref, Bo_ref) = refs[:-2], refs[-2:]
    n = ins[0].shape[0]
    for j in range(HALVES):
        h_ref, M_ref, B_ref = ins[3 * j : 3 * j + 3]
        rows = pl.ds(j * n, n)
        Co_ref[rows, :], Bo_ref[rows, :] = adagrad(M_ref[:n, :], B_ref[...], h_ref[...])


def call(kernel, operands, spaces, outs, out_spaces, scratch, mib):
    return pl.pallas_call(
        kernel,
        in_specs=[pl.BlockSpec(memory_space=s) for s in spaces],
        out_specs=[pl.BlockSpec(memory_space=s) for s in out_spaces],
        out_shape=[jax.ShapeDtypeStruct(s, f32) for s in outs],
        scratch_shapes=scratch,
        compiler_params=pltpu.CompilerParams(vmem_limit_bytes=mib << 20),
    )(*operands)


def body(tile_counts, row_counts, col_counts, row_factors, row_accum, col_factors, col_accum):
    steps = tile_counts.shape[1]
    n_outer, n_inner = lax.axis_size("outer"), lax.axis_size("inner")

    def move(block, across):
        route = [
            (o * n_inner + i, (o + across) % n_outer * n_inner + (i + 1) % n_inner)
            for o in range(n_outer)
            for i in range(n_inner)
        ]
        return lax.ppermute(block, ("outer", "inner"), route)

    rows = row_counts.reshape(-1, 128)
    cols = col_counts.reshape(1, -1)
    hbm = [tile_counts, rows, cols, row_factors, row_accum, col_factors, col_accum]
    hbm = [pltpu.with_memory_space_constraint(a, H) for a in hbm]
    wide, tall = row_factors.shape, col_factors.shape
    tile = tile_counts.shape[2:]
    half = (tall[0] // HALVES, tall[1])
    message = (half[0] + 8, half[1])
    W, A, t, c, first_grad, *blocks = call(
        first_kernel, hbm, [H] * 7,
        [wide, wide, tile, tile, half] + [message] * HALVES + [half] * HALVES, [V] * (5 + 2 * HALVES),
        [V(tile, jnp.int32), V(wide, f32), V(wide, f32), V(rows.shape, jnp.int32),
         V(cols.shape, jnp.int32), DMA((2 + HALVES + 4 + 2 * 2,)), DMA((HALVES,))],
        24,
    )
    M, B = blocks[:HALVES], blocks[HALVES:]
    for step in range(steps):
        grads = [first_grad]
        if step > 0:
            g = call(row_part_kernel, (t, c, M[0], W), [V] * 4, [wide], [V], [], 12)[0]
            operands = (t, c, M[0], M[1], W, A, g)
            if step + 1 == steps:
                W, A, *grads = call(
                    last_kernel, operands, [V] * 7, [wide, wide, half, half], [H, H, V, V],
                    [V(wide, f32), V(wide, f32), DMA((2, 2))], 20,
                )
                break
            size, halves = 512, tuple(range(HALVES))
            W, A, *grads = call(
                functools.partial(row_col_kernel, size, halves, lambda rows: None), operands, [V] * 7,
                [wide, wide] + [half] * len(halves), [V] * (2 + len(halves)), [], 20,
            )
        across = int(step + 1 == steps // 2)
        sent, sums = [], []
        for j in range(HALVES):
            if j == len(grads):
                operands = (t, c, M[j], W)
                grads += call(functools.partial(col_kernel, j), operands, [V] * 4, [half], [V], [], 12)
            value, total = call(update_kernel, (grads[j], M[j], B[j]), [V] * 3, [message, half], [V] * 2, [], 4)
            sent.append(move(value, across))
            sums.append(total)
        row_tie = lax.optimization_barrier((rows, *sums))[0]
        t, c = call(
            functools.partial(terms_kernel, step + 1), (hbm[0], row_tie), [H, V], [tile, tile], [V] * 2,
            [V(tile, jnp.int32), DMA((4,))], 12,
        )
        M, B = sent, [move(total, across) for total in sums]
    operands = (grads[0], M[0], B[0], grads[1], M[1], B[1])
    C, B = call(final_kernel, operands, [V] * 6, [tall, tall], [V] * 2, [], 6)
    return W, A, C, B


def solution(mesh):
    both = ("outer", "inner")
    return jax.shard_map(
        body,
        mesh=mesh,
        in_specs=(P(both, None, None, None), P(both), P(both)) + (P(both, None),) * 4,
        out_specs=(P(both, None),) * 4,
        check_vma=False,
    )
```

```python
import functools

import jax
import jax.numpy as jnp
from jax import lax
from jax.experimental import pallas as pl
from jax.experimental.pallas import tpu as pltpu
from jax.sharding import PartitionSpec as P


LOG_TOTAL = 17.0
LEARNING = 0.05
HALVES = 2
f32 = jnp.float32
V, H, DMA = pltpu.VMEM, pltpu.HBM, pltpu.SemaphoreType.DMA


def dot(a, b, ca, cb):
    return lax.dot_general(
        a, b, (((ca,), (cb,)), ((), ())), precision=lax.Precision.HIGH, preferred_element_type=f32
    )


def split(a):
    high = a.astype(jnp.bfloat16)
    return high, (a - high.astype(f32)).astype(jnp.bfloat16)


def split_dot(a, b, ca, cb):
    def product(p, q):
        return lax.dot_general(p, q, (((ca,), (cb,)), ((), ())), preferred_element_type=f32)

    return product(a[0], b[0]) + (product(a[0], b[1]) + product(a[1], b[0]))


def adagrad(value, total, grad):
    total = total + grad * grad
    return value - LEARNING * (grad * lax.rsqrt(total)), total


def fetches(pairs, sems):
    copies = [pltpu.make_async_copy(src, dst, sems.at[i]) for i, (src, dst) in enumerate(pairs)]
    for copy in copies:
        copy.start()
    return copies


def row_spans(n, size):
    return [pl.ds(start, size) for start in range(0, n, size)]


def put_terms(x, row_logs, first, t_ref, c_ref, rows):
    m = jnp.maximum(x.astype(f32), 1.0)
    lanes = row_logs.shape[0]
    logs = [row_logs[:, j : j + 1] for j in range(first, first + x.shape[0] // lanes)]
    t_ref[rows, :] = jnp.log(m) - jnp.concatenate(logs, axis=0)
    c_ref[rows, :] = jnp.where(x > 0, 0.1 + 0.25 * (m * lax.rsqrt(m)), 0.0)


def errors(z, target, confidence, col_logs):
    gap = (z - target) + col_logs
    return jnp.where(confidence > 0.0, confidence * gap, 0.5 * jnp.tanh(0.5 * gap) + 0.5)


def shifted_row_logs(rows_ref):
    return jnp.log(rows_ref[...].astype(f32)).T - LOG_TOTAL


def terms_kernel(step, x_hbm, rows_ref, t_ref, c_ref, x_buf, sems):
    spans = row_spans(x_buf.shape[0], 256)
    copies = fetches([(x_hbm.at[0, step, rows], x_buf.at[rows]) for rows in spans], sems)
    row_logs = shifted_row_logs(rows_ref)
    for i, rows in enumerate(spans):
        copies[i].wait()
        put_terms(x_buf[rows, :], row_logs, 2 * i, t_ref, c_ref, rows)


def first_kernel(
    x_hbm, rows_hbm, cols_hbm, W_hbm, A_hbm, C_hbm, B_hbm, Wo_ref, Ao_ref, t_ref, c_ref, h_ref, *rest
):
    M_refs, B_refs = rest[:HALVES], rest[HALVES : 2 * HALVES]
    x_buf, W_buf, A_buf, rows_buf, cols_buf, sems, late_sems = rest[2 * HALVES :]
    n, width = B_refs[0].shape
    quarters, spans = row_spans(x_buf.shape[0], 256), row_spans(x_buf.shape[0], 512)
    pairs = [(cols_hbm, cols_buf), (rows_hbm, rows_buf)]
    pairs += [(C_hbm.at[pl.ds(j * n, n)], M_refs[j].at[pl.ds(0, n)]) for j in range(HALVES)]
    head = len(pairs)
    pairs += [(x_hbm.at[0, 0, rows], x_buf.at[rows]) for rows in quarters]
    body = len(pairs)
    for rows in spans:
        pairs.append((W_hbm.at[rows], W_buf.at[rows]))
        pairs.append((A_hbm.at[rows], A_buf.at[rows]))
    copies = fetches(pairs, sems)
    late = fetches([(B_hbm.at[pl.ds(j * n, n)], B_refs[j]) for j in range(HALVES)], late_sems)
    for copy in copies[:2]:
        copy.wait()
    col_logs = jnp.log(cols_buf[...].astype(f32))
    row_logs = shifted_row_logs(rows_buf)
    for i, rows in enumerate(quarters):
        copies[head + i].wait()
        put_terms(x_buf[rows, :], row_logs, 2 * i, t_ref, c_ref, rows)
    for copy in copies[2:head]:
        copy.wait()
    for j in range(HALVES):
        M_refs[j][n:, :] = jnp.broadcast_to(col_logs[:, j * n : (j + 1) * n], (8, width))
    C = jnp.concatenate([ref[:n, :] for ref in M_refs], axis=0)
    for i, rows in enumerate(spans):
        for copy in copies[body + 2 * i : body + 2 * i + 2]:
            copy.wait()
        W = W_buf[rows, :]
        e = errors(dot(W, C, 1, 1), t_ref[rows, :], c_ref[rows, :], col_logs)
        Wo_ref[rows, :], Ao_ref[rows, :] = adagrad(W, A_buf[rows, :], dot(e, C, 1, 0))
    h_ref[...] = col_gradient((0,), t_ref, c_ref, M_refs[:1], Wo_ref)
    for copy in late:
        copy.wait()


def col_gradient(halves, t_ref, c_ref, M_refs, W_ref):
    n = M_refs[0].shape[1]
    cols = pl.ds(halves[0] * n, len(halves) * n)
    C = split(jnp.concatenate([ref[:n, :] for ref in M_refs], axis=0))
    col_logs = jnp.concatenate([ref[n : n + 1, :] for ref in M_refs], axis=1)
    grad = None
    for rows in row_spans(W_ref.shape[0], 256):
        W = split(W_ref[rows, :])
        e = errors(split_dot(W, C, 1, 1), t_ref[rows, cols], c_ref[rows, cols], col_logs)
        part = split_dot(split(e), W, 0, 0)
        grad = part if grad is None else grad + part
    return grad


def half_errors(j, W, t_ref, c_ref, M_ref, rows):
    n = M_ref.shape[1]
    cols = pl.ds(j * n, n)
    C = M_ref[:n, :]
    e = errors(dot(W, C, 1, 1), t_ref[rows, cols], c_ref[rows, cols], M_ref[n : n + 1, :])
    return e, C


def row_part_kernel(t_ref, c_ref, M_ref, W_ref, g_ref):
    for rows in row_spans(W_ref.shape[0], 256):
        e, C = half_errors(0, W_ref[rows, :], t_ref, c_ref, M_ref, rows)
        g_ref[rows, :] = dot(e, C, 1, 0)


def row_col_kernel(
    size, halves, after, t_ref, c_ref, M0_ref, M1_ref, W_ref, A_ref, g_ref, Wo_ref, Ao_ref, *h_refs
):
    for rows in row_spans(W_ref.shape[0], size):
        W = W_ref[rows, :]
        e, C = half_errors(1, W, t_ref, c_ref, M1_ref, rows)
        Wo_ref[rows, :], Ao_ref[rows, :] = adagrad(W, A_ref[rows, :], g_ref[rows, :] + dot(e, C, 1, 0))
        after(rows)
    grad = col_gradient(halves, t_ref, c_ref, (M0_ref, M1_ref)[: len(halves)], Wo_ref)
    for j, h_ref in enumerate(h_refs):
        n = h_ref.shape[0]
        h_ref[...] = grad[j * n : (j + 1) * n, :]


def last_kernel(*refs):
    ins, (Wo_hbm, Ao_hbm, h0_ref, h1_ref, W_buf, A_buf, sems) = refs[:7], refs[7:]
    stores = []

    def after(rows):
        pairs = [(W_buf.at[rows], Wo_hbm.at[rows]), (A_buf.at[rows], Ao_hbm.at[rows])]
        stores.extend(fetches(pairs, sems.at[len(stores) // 2]))

    row_col_kernel(512, (0, 1), after, *ins, W_buf, A_buf, h0_ref, h1_ref)
    for copy in stores:
        copy.wait()


def col_kernel(j, t_ref, c_ref, M_ref, W_ref, h_ref):
    h_ref[...] = col_gradient((j,), t_ref, c_ref, (M_ref,), W_ref)


def update_kernel(h_ref, M_ref, B_ref, Mo_ref, Bo_ref):
    n = h_ref.shape[0]
    Mo_ref[:n, :], Bo_ref[...] = adagrad(M_ref[:n, :], B_ref[...], h_ref[...])
    Mo_ref[n:, :] = M_ref[n:, :]


def final_kernel(*refs):
    ins, (Co_ref, Bo_ref) = refs[:-2], refs[-2:]
    n = ins[0].shape[0]
    for j in range(HALVES):
        h_ref, M_ref, B_ref = ins[3 * j : 3 * j + 3]
        rows = pl.ds(j * n, n)
        Co_ref[rows, :], Bo_ref[rows, :] = adagrad(M_ref[:n, :], B_ref[...], h_ref[...])


def call(kernel, operands, spaces, outs, out_spaces, scratch, mib):
    return pl.pallas_call(
        kernel,
        in_specs=[pl.BlockSpec(memory_space=s) for s in spaces],
        out_specs=[pl.BlockSpec(memory_space=s) for s in out_spaces],
        out_shape=[jax.ShapeDtypeStruct(s, f32) for s in outs],
        scratch_shapes=scratch,
        compiler_params=pltpu.CompilerParams(vmem_limit_bytes=mib << 20),
    )(*operands)


def body(tile_counts, row_counts, col_counts, row_factors, row_accum, col_factors, col_accum):
    steps = tile_counts.shape[1]
    n_outer, n_inner = lax.axis_size("outer"), lax.axis_size("inner")

    def move(block, across):
        route = [
            (o * n_inner + i, (o + across) % n_outer * n_inner + (i + 1) % n_inner)
            for o in range(n_outer)
            for i in range(n_inner)
        ]
        return lax.ppermute(block, ("outer", "inner"), route)

    rows = row_counts.reshape(-1, 128)
    cols = col_counts.reshape(1, -1)
    hbm = [tile_counts, rows, cols, row_factors, row_accum, col_factors, col_accum]
    hbm = [pltpu.with_memory_space_constraint(a, H) for a in hbm]
    wide, tall = row_factors.shape, col_factors.shape
    tile = tile_counts.shape[2:]
    half = (tall[0] // HALVES, tall[1])
    message = (half[0] + 8, half[1])
    W, A, t, c, first_grad, *blocks = call(
        first_kernel, hbm, [H] * 7,
        [wide, wide, tile, tile, half] + [message] * HALVES + [half] * HALVES, [V] * (5 + 2 * HALVES),
        [V(tile, jnp.int32), V(wide, f32), V(wide, f32), V(rows.shape, jnp.int32),
         V(cols.shape, jnp.int32), DMA((2 + HALVES + 4 + 2 * 2,)), DMA((HALVES,))],
        24,
    )
    M, B = blocks[:HALVES], blocks[HALVES:]
    for step in range(steps):
        grads = [first_grad]
        if step > 0:
            g = call(row_part_kernel, (t, c, M[0], W), [V] * 4, [wide], [V], [], 12)[0]
            operands = (t, c, M[0], M[1], W, A, g)
            if step + 1 == steps:
                W, A, *grads = call(
                    last_kernel, operands, [V] * 7, [wide, wide, half, half], [H, H, V, V],
                    [V(wide, f32), V(wide, f32), DMA((2, 2))], 20,
                )
                break
            size, halves = (512, (0, 1)) if step == steps // 2 else (256, (0,))
            W, A, *grads = call(
                functools.partial(row_col_kernel, size, halves, lambda rows: None), operands, [V] * 7,
                [wide, wide] + [half] * len(halves), [V] * (2 + len(halves)), [], 20,
            )
        across = int(step + 1 == steps // 2)
        sent, sums = [], []
        for j in range(HALVES):
            if j == len(grads):
                operands = (t, c, M[j], W)
                grads += call(functools.partial(col_kernel, j), operands, [V] * 4, [half], [V], [], 12)
            value, total = call(update_kernel, (grads[j], M[j], B[j]), [V] * 3, [message, half], [V] * 2, [], 4)
            sent.append(move(value, across))
            sums.append(total)
        row_tie = lax.optimization_barrier((rows, *sums))[0]
        t, c = call(
            functools.partial(terms_kernel, step + 1), (hbm[0], row_tie), [H, V], [tile, tile], [V] * 2,
            [V(tile, jnp.int32), DMA((4,))], 12,
        )
        M, B = sent, [move(total, across) for total in sums]
    operands = (grads[0], M[0], B[0], grads[1], M[1], B[1])
    C, B = call(final_kernel, operands, [V] * 6, [tall, tall], [V] * 2, [], 6)
    return W, A, C, B


def solution(mesh):
    both = ("outer", "inner")
    return jax.shard_map(
        body,
        mesh=mesh,
        in_specs=(P(both, None, None, None), P(both), P(both)) + (P(both, None),) * 4,
        out_specs=(P(both, None),) * 4,
        check_vma=False,
    )
```
